128 devices in a mesh: dp: 32 (over y_lo, z, x), mp: 4 (over y_hi, core).
Axes of the slice: x: 4, y: 4 (y_hi: 2, y_lo: 2; y = y_hi * 2 + y_lo), z: 4, core: 2. Of those that a mesh axis runs over, the one named last changes fastest.
Arguments:
- layer_inputs: bfloat16 [16384, 8192], P('dp', 'mp'), may hold values from -54 to 54
- out_grads: bfloat16 [16384, 28672], P('dp', 'mp'), may hold values from -54 to 54
- loss_mask: int32 [16384], P('dp'), may hold values 0 or 1
- start_in: int32 [64, 8192], P(None, 'mp'), may hold values from -127 to 127
- start_out: int32 [64, 28672], P(None, 'mp'), may hold values from -127 to 127
Outputs:
- features: float32 [64, 4096], P('dp', 'mp')
- basis_in: float32 [64, 8192], P(None, 'mp')
- basis_out: float32 [64, 28672], P(None, 'mp')
The draws below stay inside these ranges and needn't reach their ends.
All inputs are finite; a program needn't handle non-finite values. No bound on the sum of `loss_mask` on one device may be relied on, other than what follows from the above.
Results may differ from the reference program's by a relative error of at most 0.0065.
Values may be sent and summed in bfloat16 or wider, within the bound.
No kernel may reach another device: no remote copies, remote signals or barrier semaphores. Data moves between devices by JAX's collectives and lax.ppermute only.
A program may use at most 64 MiB of HBM per device.

```python
import math
import jax
import jax.numpy as jnp
from jax import lax

D = 8192
F = 28672
R = 64
ITERS = 2
LEN = 256
SEQS = 64
TOKENS = 16384


def scaled_field(key, rows, cols):
    keys = jax.random.split(key, 3)
    row_pos = jnp.arange(rows).astype(jnp.float32)[:, None] / rows
    col_pos = jnp.arange(cols).astype(jnp.float32)[None, :] / cols
    row_scale = jnp.exp(jax.random.uniform(keys[1], (rows, 1), jnp.float32, math.log(0.3), math.log(3.0))) * (1.0 + 2.0 * row_pos)
    col_scale = jnp.exp(jax.random.uniform(keys[2], (1, cols), jnp.float32, math.log(0.4), math.log(1.6))) * (1.0 + 1.5 * col_pos)
    base = jnp.clip(jax.random.normal(keys[0], (rows, cols), jnp.float32), -4.0, 4.0)
    return (0.25 * base * row_scale * col_scale).astype(jnp.bfloat16)


def draw_layer_inputs(key, part):
    return scaled_field(jax.random.fold_in(key, 11), TOKENS, D)


def draw_out_grads(key, part):
    return scaled_field(jax.random.fold_in(key, 23), TOKENS, F)


def place_ends(array, own_key, smallest, largest):
    extent = array.shape
    index_at = [jax.random.randint(jax.random.fold_in(own_key, axis), (), 0, extent[axis]) for axis in range(len(extent))]
    array = array.at[tuple(index_at)].set(smallest)
    longest = extent.index(max(extent))
    index_at[longest] = (index_at[longest] + 1) % extent[longest]
    return array.at[tuple(index_at)].set(largest)


def setup_inputs(seed: int = 0) -> dict:
    seeds = jax.random.split(jax.random.key(seed), 6)
    return {
        "layer_inputs": draw_layer_inputs(jax.random.fold_in(seeds[5], 71), 0),
        "out_grads": draw_out_grads(jax.random.fold_in(seeds[5], 71), 0),
        "loss_mask": place_ends((jax.random.randint(seeds[2], (TOKENS,), 0, 4) < 3).astype(jnp.int32), jax.random.fold_in(seeds[2], 1), 0, 1),
        "start_in": place_ends(jax.random.randint(seeds[3], (R, D), -127, 128), jax.random.fold_in(seeds[3], 1), -127, 127).astype(jnp.int32),
        "start_out": place_ends(jax.random.randint(seeds[4], (R, F), -127, 128), jax.random.fold_in(seeds[4], 1), -127, 127).astype(jnp.int32),
    }


def orth_step(data, basis):
    half = basis.astype(jnp.bfloat16)
    coords = lax.dot_general(data.astype(jnp.float32), half.astype(jnp.float32), (((1,), (1,)), ((), ())), preferred_element_type=jnp.float32).astype(jnp.bfloat16)
    image = lax.dot_general(coords.astype(jnp.float32), data.astype(jnp.float32), (((0,), (0,)), ((), ())), preferred_element_type=jnp.float32)
    gram = jnp.dot(image, image.T, precision=lax.Precision.HIGHEST)
    lower = jnp.linalg.cholesky(gram)
    return jax.scipy.linalg.solve_triangular(lower, image, lower=True)

def reference(layer_inputs, out_grads, loss_mask, start_in, start_out):
    masked = out_grads * loss_mask[:, None].astype(jnp.bfloat16)
    basis_in = start_in.astype(jnp.float32) / 128.0
    basis_out = start_out.astype(jnp.float32) / 128.0
    for step in range(ITERS):
        basis_in = orth_step(layer_inputs, basis_in)
        basis_out = orth_step(masked, basis_out)
    proj_in = jnp.dot(layer_inputs.astype(jnp.float32), basis_in.astype(jnp.bfloat16).T.astype(jnp.float32), preferred_element_type=jnp.float32).astype(jnp.bfloat16)
    proj_out = jnp.dot(masked.astype(jnp.float32), basis_out.astype(jnp.bfloat16).T.astype(jnp.float32), preferred_element_type=jnp.float32).astype(jnp.bfloat16)
    seq_in = proj_in.astype(jnp.float32).reshape(SEQS, LEN, R)
    seq_out = proj_out.astype(jnp.float32).reshape(SEQS, LEN, R)
    features = jnp.einsum('sti,stj->sij', seq_in, seq_out) / LEN
    return (features.reshape(SEQS, R * R), basis_in, basis_out)
```

```python
import functools

import jax
import jax.numpy as jnp
from jax import lax
from jax.experimental import pallas as pl
from jax.experimental.pallas import tpu as pltpu
from jax.sharding import PartitionSpec as P

ITERS = 2
LEN = 256
R = 64
ROWS = 16
GROUPS = R // ROWS
NT = (((1,), (1,)), ((), ()))
F32 = jnp.float32
BF16 = jnp.bfloat16


def split3(x):
    a = x.astype(BF16)
    rest = x - a.astype(F32)
    b = rest.astype(BF16)
    c = (rest - b.astype(F32)).astype(BF16)
    return jnp.concatenate([a, b, c], axis=1)


def eliminate(gram):
    n = gram.shape[0]
    col_id = lax.broadcasted_iota(jnp.int32, (n, n), 1)
    row_id = lax.broadcasted_iota(jnp.int32, (n, n), 0)
    eye = (col_id == row_id).astype(F32)
    work = jnp.concatenate([gram, eye], axis=1)
    tiles = [work[8 * i : 8 * i + 8] for i in range(n // 8)]
    sub = lax.broadcasted_iota(jnp.int32, (8, 1), 0)
    for k in range(n - 1):
        t, r = divmod(k, 8)
        row = tiles[t][r : r + 1]
        scaled = row * (1.0 / row[:, k : k + 1])
        for i in range(t, n // 8):
            col = tiles[i][:, k : k + 1]
            if i == t:
                if r == 7:
                    continue
                col = jnp.where(sub > r, col, 0.0)
            tiles[i] = tiles[i] - col * scaled
    work = jnp.concatenate(tiles, axis=0)
    diag = jnp.sum(jnp.where(col_id == row_id, work[:, :n], 0.0), axis=1, keepdims=True)
    return work[:, n:] * (1.0 / jnp.sqrt(diag))


def raw_kernel(first, steps, core, *refs):
    if first:
        bin_ref, bout_ref, min_ref, mout_ref, mask_ref, send, keep, acc = refs
    else:
        img_ref, min_ref, mout_ref, mask_ref, send, keep, acc, gin, gout = refs
    h = pl.program_id(0)

    @pl.when(h == 0)
    def _():
        acc[...] = jnp.zeros_like(acc)
        if not first:
            gin[...] = jnp.zeros_like(gin)
            gout[...] = jnp.zeros_like(gout)

    if first:
        half_in = (bin_ref[...].astype(F32) * (1.0 / 128.0)).astype(BF16)
        half_out = (bout_ref[...].astype(F32) * (1.0 / 128.0)).astype(BF16)
    else:
        wide = min_ref.shape[1]
        img = jnp.concatenate([img_ref[g, 0] for g in range(GROUPS)], axis=0)
        half_in = img[:, :wide]
        half_out = img[:, wide:]
        gin[...] += lax.dot_general(half_in, half_in, NT, preferred_element_type=F32)
        gout[...] += lax.dot_general(half_out, half_out, NT, preferred_element_type=F32)
    acc[:R] += lax.dot_general(half_in, min_ref[...], NT, preferred_element_type=F32)
    acc[R:] += lax.dot_general(half_out, mout_ref[...], NT, preferred_element_type=F32)

    @pl.when(h == steps - 1)
    def _():
        tokens = acc.shape[1] // 2
        mask = mask_ref[...].astype(F32)
        acc[R:] = acc[R:] * mask
        mine = pl.ds(pl.multiple_of(core[0] * tokens, tokens), tokens)
        other = pl.ds(pl.multiple_of((1 - core[0]) * tokens, tokens), tokens)
        keep[: 2 * R] = acc[:, mine]
        send[: 2 * R] = acc[:, other]
        if not first:
            gram = jnp.concatenate([gin[...], gout[...]], axis=1)
            gram = jnp.concatenate([gram[: R // 2], gram[R // 2 :]], axis=1)
            keep[2 * R :] = gram
            send[2 * R :] = gram


def raw_coords(core, image, layer_inputs, out_grads, mask, starts=None):
    first = image is None
    steps = 8
    rows, d_in = layer_inputs.shape
    d_out = out_grads.shape[1]
    w_in, w_out = d_in // steps, d_out // steps
    if first:
        lead = list(starts)
        lead_specs = [
            pl.BlockSpec((R, w_in), lambda h, c: (0, h)),
            pl.BlockSpec((R, w_out), lambda h, c: (0, h)),
        ]
    else:
        lead = [image]
        lead_specs = [pl.BlockSpec((GROUPS, 1, ROWS, w_in + w_out), lambda h, c: (0, h, 0, 0))]
    height = 2 * R if first else 2 * R + R // 2
    shape = jax.ShapeDtypeStruct((height, rows // 2), F32)
    whole = pl.BlockSpec((height, rows // 2), lambda h, c: (0, 0))
    scratch = [pltpu.VMEM((2 * R, rows), F32)]
    if not first:
        scratch += [pltpu.VMEM((R, R), F32)] * 2
    return pl.pallas_call(
        functools.partial(raw_kernel, first, steps),
        out_shape=(shape, shape),
        grid_spec=pltpu.PrefetchScalarGridSpec(
            num_scalar_prefetch=1,
            grid=(steps,),
            in_specs=lead_specs
            + [
                pl.BlockSpec((rows, w_in), lambda h, c: (0, h)),
                pl.BlockSpec((rows, w_out), lambda h, c: (0, h)),
                pl.BlockSpec((1, rows), lambda h, c: (0, 0)),
            ],
            out_specs=(whole, whole),
            scratch_shapes=scratch,
        ),
        name="raw_first" if first else "raw_next",
    )(core, *lead, layer_inputs, out_grads, mask)


def image_kernel(core, mine_ref, other_ref, min_ref, mout_ref, out, coords):
    tokens = mine_ref.shape[1]

    @pl.when(pl.program_id(0) == 0)
    def _():
        coords[:, pl.ds(pl.multiple_of(core[0] * tokens, tokens), tokens)] = mine_ref[...]
        coords[:, pl.ds(pl.multiple_of((1 - core[0]) * tokens, tokens), tokens)] = other_ref[...]

    wide = min_ref.shape[1]
    part_in = jnp.dot(coords[:R], min_ref[...], preferred_element_type=F32).astype(BF16)
    part_out = jnp.dot(coords[R:], mout_ref[...], preferred_element_type=F32).astype(BF16)
    for g in range(GROUPS):
        out[g, 0, :, :wide] = part_in[g * ROWS : (g + 1) * ROWS]
        out[g, 0, :, wide:] = part_out[g * ROWS : (g + 1) * ROWS]


def image_of(core, mine, other, layer_inputs, out_grads):
    steps = 8
    rows, d_in = layer_inputs.shape
    d_out = out_grads.shape[1]
    w_in, w_out = d_in // steps, d_out // steps
    whole = pl.BlockSpec((2 * R, rows // 2), lambda h, c: (0, 0))
    return pl.pallas_call(
        image_kernel,
        out_shape=jax.ShapeDtypeStruct((GROUPS, steps, ROWS, w_in + w_out), BF16),
        grid_spec=pltpu.PrefetchScalarGridSpec(
            num_scalar_prefetch=1,
            grid=(steps,),
            in_specs=[
                whole,
                whole,
                pl.BlockSpec((rows, w_in), lambda h, c: (0, h)),
                pl.BlockSpec((rows, w_out), lambda h, c: (0, h)),
            ],
            out_specs=pl.BlockSpec((GROUPS, 1, ROWS, w_in + w_out), lambda h, c: (0, h, 0, 0)),
            scratch_shapes=[pltpu.VMEM((2 * R, rows), BF16)],
        ),
        name="image",
    )(core, mine, other, layer_inputs, out_grads)


def sum_kernel(parts, out):
    total = parts[0].astype(F32)
    for i in range(1, parts.shape[0]):
        total = total + parts[i].astype(F32)
    half = total.astype(BF16)
    for i in range(parts.shape[0]):
        out[i] = half


def sum_copies(parts):
    return pl.pallas_call(
        sum_kernel,
        out_shape=jax.ShapeDtypeStruct(parts.shape, parts.dtype),
        name="sum_copies",
    )(parts)


def solve_kernel(last, near, far, *refs):
    total = near[...] + far[...]
    gram = total[2 * R :]
    half = gram.shape[1] // 2
    gram = jnp.concatenate([gram[:, :half], gram[:, half:]], axis=0)
    inv_in = eliminate(gram[:, :R])
    inv_out = eliminate(gram[:, R:])
    high = lax.Precision.HIGHEST
    co_in = jnp.dot(inv_in, total[:R], precision=high, preferred_element_type=F32)
    co_out = jnp.dot(inv_out, total[R : 2 * R], precision=high, preferred_element_type=F32)
    if last:
        feat, split = refs
        feat[...] = lax.dot_general(
            co_in.astype(BF16), co_out.astype(BF16), NT, preferred_element_type=F32
        ) * (1.0 / LEN)
        split[0] = split3(inv_in)
        split[1] = split3(inv_out)
    else:
        (coords,) = refs
        coords[:R] = co_in.astype(BF16)
        coords[R:] = co_out.astype(BF16)


def solve(near, far, last):
    if last:
        shape = (
            jax.ShapeDtypeStruct((R, R), F32),
            jax.ShapeDtypeStruct((2, R, 3 * R), BF16),
        )
    else:
        shape = jax.ShapeDtypeStruct((2 * R, near.shape[1]), BF16)
    return pl.pallas_call(
        functools.partial(solve_kernel, last),
        out_shape=shape,
        name="solve_last" if last else "solve",
    )(near, far)


def basis_kernel(split, img_ref, in_ref, out_ref):
    wide = in_ref.shape[1]
    img = jnp.concatenate([img_ref[g, 0] for g in range(GROUPS)] * 3, axis=0)
    in_ref[...] = jnp.dot(split[0], img[:, :wide], preferred_element_type=F32)
    out_ref[...] = jnp.dot(split[1], img[:, wide:], preferred_element_type=F32)


def basis_of(split, image, d_in, d_out):
    steps = image.shape[1]
    w_in, w_out = d_in // steps, d_out // steps
    return pl.pallas_call(
        basis_kernel,
        out_shape=(jax.ShapeDtypeStruct((R, d_in), F32), jax.ShapeDtypeStruct((R, d_out), F32)),
        grid=(steps,),
        in_specs=[
            pl.BlockSpec(split.shape, lambda h: (0, 0, 0)),
            pl.BlockSpec((GROUPS, 1, ROWS, w_in + w_out), lambda h: (0, h, 0, 0)),
        ],
        out_specs=(
            pl.BlockSpec((R, w_in), lambda h: (0, h)),
            pl.BlockSpec((R, w_out), lambda h: (0, h)),
        ),
        name="basis",
    )(split, image)


CORE_SWAP = [(0, 1), (1, 0), (2, 3), (3, 2)]
CHIP_SWAP = [(0, 2), (2, 0), (1, 3), (3, 1)]


def shards(layer_inputs, out_grads, loss_mask, start_in, start_out):
    mp = lax.axis_index("mp")
    core = (mp % 2).reshape(1)
    mask = loss_mask.reshape(1, -1)

    def exchange(send, keep):
        near = keep + lax.ppermute(send, "mp", CORE_SWAP)
        return near, lax.ppermute(near, "mp", CHIP_SWAP)

    send, keep = raw_coords(core, None, layer_inputs, out_grads, mask, (start_in, start_out))
    near, far = exchange(send, keep)
    mine = (near + far).astype(BF16)
    for step in range(ITERS):
        other = lax.ppermute(mine, "mp", CORE_SWAP)
        parts = image_of(core, mine, other, layer_inputs, out_grads)
        grid = parts.shape
        parts = parts.reshape(grid[0] * grid[1], grid[2], grid[3])
        parts = lax.all_to_all(parts, "dp", 0, 0)
        image = lax.all_to_all(sum_copies(parts), "dp", 0, 0).reshape(grid)
        send, keep = raw_coords(core, image, layer_inputs, out_grads, mask)
        near, far = exchange(send, keep)
        if step + 1 < ITERS:
            mine = solve(near, far, False)
    feat, split = solve(near, far, True)
    basis_in, basis_out = basis_of(split, image, layer_inputs.shape[1], out_grads.shape[1])
    block = R // lax.axis_size("mp")
    own = lax.dynamic_slice_in_dim(feat, mp * block, block, 0)
    theirs = lax.dynamic_slice_in_dim(feat, (mp + 1 - 2 * (mp % 2)) * block, block, 0)
    got = lax.ppermute(theirs, "mp", CORE_SWAP)
    own, got = own.reshape(1, -1), got.reshape(1, -1)
    even = mp % 2 == 0
    features = jnp.concatenate([jnp.where(even, own, got), jnp.where(even, got, own)], axis=0)
    return (features, basis_in, basis_out)


def solution(mesh):
    in_specs = (P("dp", "mp"), P("dp", "mp"), P("dp"), P(None, "mp"), P(None, "mp"))
    out_specs = (P("dp", "mp"), P(None, "mp"), P(None, "mp"))
    return jax.shard_map(shards, mesh=mesh, in_specs=in_specs, out_specs=out_specs, check_vma=False)
```

```python
import functools

import jax
import jax.numpy as jnp
from jax import lax
from jax.experimental import pallas as pl
from jax.experimental.pallas import tpu as pltpu
from jax.sharding import PartitionSpec as P

ITERS = 2
LEN = 256
R = 64
ROWS = 16
GROUPS = R // ROWS
NT = (((1,), (1,)), ((), ()))
F32 = jnp.float32
BF16 = jnp.bfloat16


def split3(x):
    a = x.astype(BF16)
    rest = x - a.astype(F32)
    b = rest.astype(BF16)
    c = (rest - b.astype(F32)).astype(BF16)
    return jnp.concatenate([a, b, c], axis=1)


def eliminate(gram):
    n = gram.shape[0]
    col_id = lax.broadcasted_iota(jnp.int32, (n, n), 1)
    row_id = lax.broadcasted_iota(jnp.int32, (n, n), 0)
    eye = (col_id == row_id).astype(F32)
    work = jnp.concatenate([gram, eye], axis=1)
    tiles = [work[8 * i : 8 * i + 8] for i in range(n // 8)]
    sub = lax.broadcasted_iota(jnp.int32, (8, 1), 0)
    for k in range(n - 1):
        t, r = divmod(k, 8)
        row = tiles[t][r : r + 1]
        scaled = row * (1.0 / row[:, k : k + 1])
        for i in range(t, n // 8):
            col = tiles[i][:, k : k + 1]
            if i == t:
                if r == 7:
                    continue
                col = jnp.where(sub > r, col, 0.0)
            tiles[i] = tiles[i] - col * scaled
    work = jnp.concatenate(tiles, axis=0)
    diag = jnp.sum(jnp.where(col_id == row_id, work[:, :n], 0.0), axis=1, keepdims=True)
    return work[:, n:] * (1.0 / jnp.sqrt(diag))


def params(mib):
    return pltpu.CompilerParams(vmem_limit_bytes=mib << 20)


VMEM = pl.BlockSpec(memory_space=pltpu.VMEM)
SMEM = pl.BlockSpec(memory_space=pltpu.SMEM)
HBM = pl.BlockSpec(memory_space=pltpu.HBM)


def halves(place, tokens):
    core = place[0] & 1
    mine = pl.ds(pl.multiple_of(core * tokens, tokens), tokens)
    other = pl.ds(pl.multiple_of((1 - core) * tokens, tokens), tokens)
    return mine, other


def first_kernel(place, bin_hbm, bout_hbm, min_hbm, mout_hbm, mask_hbm, *refs):
    send, keep, mins, mouts, mask, bins, bouts, ints, acc, sems, mask_sem = refs
    steps = sems.shape[0]
    pairs = ((bin_hbm, bins), (min_hbm, mins), (bout_hbm, bouts), (mout_hbm, mouts))

    def columns(ref, h):
        width = ref.shape[1] // steps
        return slice(h * width, (h + 1) * width)

    copies = []
    for h in range(steps):
        for n, (src, dst) in enumerate(pairs):
            cols = columns(dst, h)
            copy = pltpu.make_async_copy(src.at[:, cols], dst.at[:, cols], sems.at[h, n])
            copy.start()
            copies.append(copy)
    mask_copy = pltpu.make_async_copy(mask_hbm, ints, mask_sem)
    mask_copy.start()
    for h in range(steps):
        for n, (base, basis, data) in enumerate([(0, bins, mins), (R, bouts, mouts)]):
            copies[4 * h + 2 * n].wait()
            copies[4 * h + 2 * n + 1].wait()
            cols = columns(basis, h)
            half = (basis[:, cols].astype(F32) * (1.0 / 128.0)).astype(BF16)
            part = lax.dot_general(half, data[:, cols], NT, preferred_element_type=F32)
            if h == 0:
                acc[base : base + R] = part
            else:
                acc[base : base + R] += part
    mask_copy.wait()
    mask[...] = ints[...].astype(F32)
    acc[R:] = acc[R:] * mask[...]
    mine, other = halves(place, acc.shape[1] // 2)
    keep[...] = acc[:, mine]
    send[...] = acc[:, other]


def raw_first(place, *whole):
    start_in, start_out, layer_inputs, out_grads, mask = whole
    rows = layer_inputs.shape[0]
    shape = jax.ShapeDtypeStruct((2 * R, rows // 2), F32)
    return pl.pallas_call(
        first_kernel,
        out_shape=(
            shape,
            shape,
            jax.ShapeDtypeStruct(layer_inputs.shape, BF16),
            jax.ShapeDtypeStruct(out_grads.shape, BF16),
            jax.ShapeDtypeStruct(mask.shape, F32),
        ),
        in_specs=[SMEM, HBM, HBM, HBM, HBM, HBM],
        out_specs=(VMEM,) * 5,
        scratch_shapes=[
            pltpu.VMEM(start_in.shape, jnp.int32),
            pltpu.VMEM(start_out.shape, jnp.int32),
            pltpu.VMEM(mask.shape, jnp.int32),
            pltpu.VMEM((2 * R, rows), F32),
            pltpu.SemaphoreType.DMA((8, 4)),
            pltpu.SemaphoreType.DMA,
        ],
        compiler_params=params(8),
        name="raw_first",
    )(place, *(pltpu.with_memory_space_constraint(x, pltpu.HBM) for x in whole))


def next_kernel(place, img_ref, min_ref, mout_ref, mask_ref, send, keep, img_in, img_out, acc):
    steps = img_ref.shape[1]
    w_in = img_in.shape[1] // steps
    w_out = img_out.shape[1] // steps
    for h in range(steps):
        for g in range(GROUPS):
            rows = slice(g * ROWS, (g + 1) * ROWS)
            img_in[rows, h * w_in : (h + 1) * w_in] = img_ref[g, h, :, :w_in]
            img_out[rows, h * w_out : (h + 1) * w_out] = img_ref[g, h, :, w_in:]
    half_in, half_out = img_in[...], img_out[...]
    gram_in = lax.dot_general(half_in, half_in, NT, preferred_element_type=F32)
    gram_out = lax.dot_general(half_out, half_out, NT, preferred_element_type=F32)
    acc[:R] = lax.dot_general(half_in, min_ref[...], NT, preferred_element_type=F32)
    raw_out = lax.dot_general(half_out, mout_ref[...], NT, preferred_element_type=F32)
    acc[R:] = raw_out * mask_ref[...]
    mine, other = halves(place, acc.shape[1] // 2)
    keep[: 2 * R] = acc[:, mine]
    send[: 2 * R] = acc[:, other]
    gram = jnp.concatenate([gram_in, gram_out], axis=1)
    gram = jnp.concatenate([gram[: R // 2], gram[R // 2 :]], axis=1)
    keep[2 * R :] = gram
    send[2 * R :] = gram


def raw_next(place, image, layer_inputs, out_grads, mask):
    rows, d_in = layer_inputs.shape
    d_out = out_grads.shape[1]
    shape = jax.ShapeDtypeStruct((2 * R + R // 2, rows // 2), F32)
    return pl.pallas_call(
        next_kernel,
        out_shape=(shape, shape),
        in_specs=[SMEM, VMEM, VMEM, VMEM, VMEM],
        out_specs=(VMEM, VMEM),
        scratch_shapes=[
            pltpu.VMEM((R, d_in), BF16),
            pltpu.VMEM((R, d_out), BF16),
            pltpu.VMEM((2 * R, rows), F32),
        ],
        compiler_params=params(8),
        name="raw_next",
    )(place, image, layer_inputs, out_grads, mask)


def add_kernel(a, b, out):
    out[...] = (a[...] + b[...]).astype(out.dtype)


def add(a, b, dtype=F32):
    return pl.pallas_call(
        add_kernel,
        out_shape=jax.ShapeDtypeStruct(a.shape, dtype),
        in_specs=[VMEM, VMEM],
        out_specs=VMEM,
        compiler_params=params(4),
        name="add",
    )(a, b)


def image_kernel(place, mine_ref, other_ref, min_ref, mout_ref, out, coords):
    mine, other = halves(place, mine_ref.shape[1])
    coords[:, mine] = mine_ref[...]
    coords[:, other] = other_ref[...]
    steps = out.shape[1]
    w_in = min_ref.shape[1] // steps
    w_out = mout_ref.shape[1] // steps
    part_in = jnp.dot(coords[:R], min_ref[...], preferred_element_type=F32).astype(BF16)
    part_out = jnp.dot(coords[R:], mout_ref[...], preferred_element_type=F32).astype(BF16)
    for h in range(steps):
        for g in range(GROUPS):
            rows = slice(g * ROWS, (g + 1) * ROWS)
            out[g, h, :, :w_in] = part_in[rows, h * w_in : (h + 1) * w_in]
            out[g, h, :, w_in:] = part_out[rows, h * w_out : (h + 1) * w_out]


def image_of(place, mine, other, layer_inputs, out_grads):
    steps = 8
    rows, d_in = layer_inputs.shape
    width = (d_in + out_grads.shape[1]) // steps
    return pl.pallas_call(
        image_kernel,
        out_shape=jax.ShapeDtypeStruct((GROUPS, steps, ROWS, width), BF16),
        in_specs=[SMEM, VMEM, VMEM, VMEM, VMEM],
        out_specs=VMEM,
        scratch_shapes=[pltpu.VMEM((2 * R, rows), BF16)],
        compiler_params=params(8),
        name="image",
    )(place, mine, other, layer_inputs, out_grads)


def sum_kernel(parts, out):
    total = parts[0].astype(F32)
    for i in range(1, parts.shape[0]):
        total = total + parts[i].astype(F32)
    half = total.astype(BF16)
    for i in range(parts.shape[0]):
        out[i] = half


def sum_copies(parts):
    return pl.pallas_call(
        sum_kernel,
        out_shape=jax.ShapeDtypeStruct(parts.shape, parts.dtype),
        in_specs=[VMEM],
        out_specs=VMEM,
        compiler_params=params(4),
        name="sum_copies",
    )(parts)


def solve_kernel(last, place, near, far, *refs):
    total = near[...] + far[...]
    gram = total[2 * R :]
    half = gram.shape[1] // 2
    gram = jnp.concatenate([gram[:, :half], gram[:, half:]], axis=0)
    inv_in = eliminate(gram[:, :R])
    inv_out = eliminate(gram[:, R:])
    high = lax.Precision.HIGHEST
    co_in = jnp.dot(inv_in, total[:R], precision=high, preferred_element_type=F32)
    co_out = jnp.dot(inv_out, total[R : 2 * R], precision=high, preferred_element_type=F32)
    if last:
        own, theirs, split, feat = refs
        feat[...] = lax.dot_general(
            co_in.astype(BF16), co_out.astype(BF16), NT, preferred_element_type=F32
        ) * (1.0 / LEN)
        rows = own.shape[0]
        own[...] = feat[pl.ds(pl.multiple_of(place[0] * rows, rows), rows)]
        theirs[...] = feat[pl.ds(pl.multiple_of((place[0] ^ 1) * rows, rows), rows)]
        split[0] = split3(inv_in)
        split[1] = split3(inv_out)
    else:
        (coords,) = refs
        coords[:R] = co_in.astype(BF16)
        coords[R:] = co_out.astype(BF16)


def solve(place, near, far, count):
    last = count is not None
    if last:
        block = jax.ShapeDtypeStruct((R // count, R), F32)
        shape = (block, block, jax.ShapeDtypeStruct((2, R, 3 * R), BF16))
    else:
        shape = jax.ShapeDtypeStruct((2 * R, near.shape[1]), BF16)
    return pl.pallas_call(
        functools.partial(solve_kernel, last),
        out_shape=shape,
        in_specs=[SMEM, VMEM, VMEM],
        out_specs=(VMEM,) * 3 if last else VMEM,
        scratch_shapes=[pltpu.VMEM((R, R), F32)] if last else [],
        compiler_params=params(8),
        name="solve_last" if last else "solve",
    )(place, near, far)


def features_kernel(place, own, got, out):
    rows = own.shape[0]
    own = jnp.concatenate([own[r : r + 1] for r in range(rows)], axis=1)
    got = jnp.concatenate([got[r : r + 1] for r in range(rows)], axis=1)
    even = (place[0] & 1) == 0
    out[0:1] = jnp.where(even, own, got)
    out[1:2] = jnp.where(even, got, own)


def features_of(place, own, got):
    return pl.pallas_call(
        features_kernel,
        out_shape=jax.ShapeDtypeStruct((2, own.size), F32),
        in_specs=[SMEM, VMEM, VMEM],
        out_specs=VMEM,
        compiler_params=params(4),
        name="features",
    )(place, own, got)


def basis_kernel(split, img_ref, in_hbm, out_hbm, b_in, b_out, sems):
    steps = img_ref.shape[1]
    w_in = b_in.shape[1] // steps
    w_out = b_out.shape[1] // steps
    copies = []
    for h in range(steps):
        img = jnp.concatenate([img_ref[g, h] for g in range(GROUPS)] * 3, axis=0)
        cols_in = slice(h * w_in, (h + 1) * w_in)
        cols_out = slice(h * w_out, (h + 1) * w_out)
        b_in[:, cols_in] = jnp.dot(split[0], img[:, :w_in], preferred_element_type=F32)
        b_out[:, cols_out] = jnp.dot(split[1], img[:, w_in:], preferred_element_type=F32)
        for n, (src, dst, cols) in enumerate([(b_in, in_hbm, cols_in), (b_out, out_hbm, cols_out)]):
            copy = pltpu.make_async_copy(src.at[:, cols], dst.at[:, cols], sems.at[h, n])
            copy.start()
            copies.append(copy)
    for copy in copies:
        copy.wait()


def basis_of(split, image, d_in, d_out):
    shapes = ((R, d_in), (R, d_out))
    return pl.pallas_call(
        basis_kernel,
        out_shape=tuple(jax.ShapeDtypeStruct(s, F32) for s in shapes),
        in_specs=[VMEM, VMEM],
        out_specs=(HBM, HBM),
        scratch_shapes=[pltpu.VMEM(s, F32) for s in shapes]
        + [pltpu.SemaphoreType.DMA((image.shape[1], 2))],
        compiler_params=params(8),
        name="basis",
    )(split, image)


CORE_SWAP = [(0, 1), (1, 0), (2, 3), (3, 2)]
CHIP_SWAP = [(0, 2), (2, 0), (1, 3), (3, 1)]


def shards(layer_inputs, out_grads, loss_mask, start_in, start_out):
    place = lax.axis_index("mp").reshape(1)
    mask = loss_mask.reshape(1, -1)
    d_in, d_out = layer_inputs.shape[1], out_grads.shape[1]

    def exchange(send, keep):
        near = add(keep, lax.ppermute(send, "mp", CORE_SWAP))
        return near, lax.ppermute(near, "mp", CHIP_SWAP)

    send, keep, layer_inputs, out_grads, mask = raw_first(
        place, start_in, start_out, layer_inputs, out_grads, mask
    )
    near, far = exchange(send, keep)
    mine = add(near, far, BF16)
    for step in range(ITERS):
        other = lax.ppermute(mine, "mp", CORE_SWAP)
        parts = image_of(place, mine, other, layer_inputs, out_grads)
        grid = parts.shape
        parts = parts.reshape(grid[0] * grid[1], grid[2], grid[3])
        parts = lax.all_to_all(parts, "dp", 0, 0)
        image = lax.all_to_all(sum_copies(parts), "dp", 0, 0).reshape(grid)
        send, keep = raw_next(place, image, layer_inputs, out_grads, mask)
        near, far = exchange(send, keep)
        if step + 1 < ITERS:
            mine = solve(place, near, far, None)
    own, theirs, split = solve(place, near, far, lax.axis_size("mp"))
    got = lax.ppermute(theirs, "mp", CORE_SWAP)
    basis_in, basis_out = basis_of(split, image, d_in, d_out)
    return (features_of(place, own, got), basis_in, basis_out)


def solution(mesh):
    in_specs = (P("dp", "mp"), P("dp", "mp"), P("dp"), P(None, "mp"), P(None, "mp"))
    out_specs = (P("dp", "mp"), P(None, "mp"), P(None, "mp"))
    return jax.shard_map(shards, mesh=mesh, in_specs=in_specs, out_specs=out_specs, check_vma=False)
```

```python
import functools

import jax
import jax.numpy as jnp
from jax import lax
from jax.experimental import pallas as pl
from jax.experimental.pallas import tpu as pltpu
from jax.sharding import PartitionSpec as P

ITERS = 2
LEN = 256
R = 64
ROWS = 16
GROUPS = R // ROWS
NT = (((1,), (1,)), ((), ()))
F32 = jnp.float32
BF16 = jnp.bfloat16


def split3(x):
    a = x.astype(BF16)
    rest = x - a.astype(F32)
    b = rest.astype(BF16)
    c = (rest - b.astype(F32)).astype(BF16)
    return jnp.concatenate([a, b, c], axis=1)


PIVOTS = 4


def eliminate(grams, size=PIVOTS):
    n = grams[0].shape[0]
    col_id = lax.broadcasted_iota(jnp.int32, (n, n), 1)
    row_id = lax.broadcasted_iota(jnp.int32, (n, n), 0)
    eye = (col_id == row_id).astype(F32)
    sub = lax.broadcasted_iota(jnp.int32, (8, 1), 0)
    works = []
    for gram in grams:
        work = jnp.concatenate([gram, eye], axis=1)
        works.append([work[8 * i : 8 * i + 8] for i in range(n // 8)])
    for k in range(0, n, size):
        t, r = divmod(k, 8)
        for tiles in works:
            rows = [tiles[t][r + i : r + i + 1] for i in range(size)]
            wide = rows[0].shape
            p = {
                (i, j): jnp.broadcast_to(rows[i][:, k + j : k + j + 1], wide)
                for i in range(size)
                for j in range(i, size)
            }
            inv, low = [], {}
            for i in range(size):
                inv.append(1.0 / p[i, i])
                for j in range(i + 1, size):
                    low[j, i] = p[i, j] * inv[i]
                for j in range(i + 1, size):
                    for m in range(j, size):
                        p[j, m] = p[j, m] - low[j, i] * p[i, m]
                    rows[j] = rows[j] - low[j, i] * rows[i]
            s = [None] * size
            for i in reversed(range(size)):
                s[i] = rows[i] * inv[i]
                for j in range(i + 1, size):
                    s[i] = s[i] - low[j, i] * s[j]
            for i in range(t, n // 8):
                tile = tiles[i]
                if i == t:
                    new = tile
                    if r + size < 8:
                        for j in range(size):
                            col = jnp.where(sub >= r + size, tile[:, k + j : k + j + 1], 0.0)
                            new = new - col * s[j]
                    for j in range(1, size):
                        new = jnp.where(sub == r + j, rows[j], new)
                    tiles[i] = new
                else:
                    new = tile
                    for j in range(size):
                        new = new - tile[:, k + j : k + j + 1] * s[j]
                    tiles[i] = new
    out = []
    for tiles in works:
        work = jnp.concatenate(tiles, axis=0)
        diag = jnp.sum(jnp.where(col_id == row_id, work[:, :n], 0.0), axis=1, keepdims=True)
        out.append(work[:, n:] * (1.0 / jnp.sqrt(diag)))
    return out


def params(mib):
    return pltpu.CompilerParams(vmem_limit_bytes=mib << 20)


VMEM = pl.BlockSpec(memory_space=pltpu.VMEM)
SMEM = pl.BlockSpec(memory_space=pltpu.SMEM)
HBM = pl.BlockSpec(memory_space=pltpu.HBM)


def halves(place, tokens):
    core = place[0] & 1
    mine = pl.ds(pl.multiple_of(core * tokens, tokens), tokens)
    other = pl.ds(pl.multiple_of((1 - core) * tokens, tokens), tokens)
    return mine, other


def first_kernel(place, bin_hbm, bout_hbm, min_hbm, mout_hbm, mask_hbm, *refs):
    send, keep, mins, mouts, mask, bins, bouts, ints, acc, sems, mask_sem = refs
    steps = sems.shape[0]
    pairs = ((bin_hbm, bins), (min_hbm, mins), (bout_hbm, bouts), (mout_hbm, mouts))

    def columns(ref, h):
        width = ref.shape[1] // steps
        return slice(h * width, (h + 1) * width)

    copies = []
    for h in range(steps):
        for n, (src, dst) in enumerate(pairs):
            cols = columns(dst, h)
            copy = pltpu.make_async_copy(src.at[:, cols], dst.at[:, cols], sems.at[h, n])
            copy.start()
            copies.append(copy)
    mask_copy = pltpu.make_async_copy(mask_hbm, ints, mask_sem)
    mask_copy.start()
    for h in range(steps):
        for n, (base, basis, data) in enumerate([(0, bins, mins), (R, bouts, mouts)]):
            copies[4 * h + 2 * n].wait()
            copies[4 * h + 2 * n + 1].wait()
            cols = columns(basis, h)
            half = (basis[:, cols].astype(F32) * (1.0 / 128.0)).astype(BF16)
            part = lax.dot_general(half, data[:, cols], NT, preferred_element_type=F32)
            if h == 0:
                acc[base : base + R] = part
            else:
                acc[base : base + R] += part
    mask_copy.wait()
    mask[...] = ints[...].astype(F32)
    acc[R:] = acc[R:] * mask[...]
    mine, other = halves(place, acc.shape[1] // 2)
    keep[...] = acc[:, mine]
    send[...] = acc[:, other]


def raw_first(place, *whole):
    start_in, start_out, layer_inputs, out_grads, mask = whole
    rows = layer_inputs.shape[0]
    shape = jax.ShapeDtypeStruct((2 * R, rows // 2), F32)
    return pl.pallas_call(
        first_kernel,
        out_shape=(
            shape,
            shape,
            jax.ShapeDtypeStruct(layer_inputs.shape, BF16),
            jax.ShapeDtypeStruct(out_grads.shape, BF16),
            jax.ShapeDtypeStruct(mask.shape, F32),
        ),
        in_specs=[SMEM, HBM, HBM, HBM, HBM, HBM],
        out_specs=(VMEM,) * 5,
        scratch_shapes=[
            pltpu.VMEM(start_in.shape, jnp.int32),
            pltpu.VMEM(start_out.shape, jnp.int32),
            pltpu.VMEM(mask.shape, jnp.int32),
            pltpu.VMEM((2 * R, rows), F32),
            pltpu.SemaphoreType.DMA((8, 4)),
            pltpu.SemaphoreType.DMA,
        ],
        compiler_params=params(8),
        name="raw_first",
    )(place, *(pltpu.with_memory_space_constraint(x, pltpu.HBM) for x in whole))


def next_kernel(place, img_ref, min_ref, mout_ref, mask_ref, send, keep, img_in, img_out, acc):
    steps = img_ref.shape[1]
    w_in = img_in.shape[1] // steps
    w_out = img_out.shape[1] // steps
    for h in range(steps):
        for g in range(GROUPS):
            rows = slice(g * ROWS, (g + 1) * ROWS)
            img_in[rows, h * w_in : (h + 1) * w_in] = img_ref[g, h, :, :w_in]
            img_out[rows, h * w_out : (h + 1) * w_out] = img_ref[g, h, :, w_in:]
    half_in, half_out = img_in[...], img_out[...]
    gram_in = lax.dot_general(half_in, half_in, NT, preferred_element_type=F32)
    gram_out = lax.dot_general(half_out, half_out, NT, preferred_element_type=F32)
    acc[:R] = lax.dot_general(half_in, min_ref[...], NT, preferred_element_type=F32)
    raw_out = lax.dot_general(half_out, mout_ref[...], NT, preferred_element_type=F32)
    acc[R:] = raw_out * mask_ref[...]
    mine, other = halves(place, acc.shape[1] // 2)
    keep[: 2 * R] = acc[:, mine]
    send[: 2 * R] = acc[:, other]
    gram = jnp.concatenate([gram_in, gram_out], axis=1)
    gram = jnp.concatenate([gram[: R // 2], gram[R // 2 :]], axis=1)
    keep[2 * R :] = gram
    send[2 * R :] = gram


def raw_next(place, image, layer_inputs, out_grads, mask):
    rows, d_in = layer_inputs.shape
    d_out = out_grads.shape[1]
    shape = jax.ShapeDtypeStruct((2 * R + R // 2, rows // 2), F32)
    return pl.pallas_call(
        next_kernel,
        out_shape=(shape, shape),
        in_specs=[SMEM, VMEM, VMEM, VMEM, VMEM],
        out_specs=(VMEM, VMEM),
        scratch_shapes=[
            pltpu.VMEM((R, d_in), BF16),
            pltpu.VMEM((R, d_out), BF16),
            pltpu.VMEM((2 * R, rows), F32),
        ],
        compiler_params=params(8),
        name="raw_next",
    )(place, image, layer_inputs, out_grads, mask)


def add_kernel(a, b, out):
    out[...] = (a[...] + b[...]).astype(out.dtype)


def add(a, b, dtype=F32):
    return pl.pallas_call(
        add_kernel,
        out_shape=jax.ShapeDtypeStruct(a.shape, dtype),
        in_specs=[VMEM, VMEM],
        out_specs=VMEM,
        compiler_params=params(4),
        name="add",
    )(a, b)


def image_kernel(place, *refs):
    *parts, mine_ref, other_ref, min_ref, mout_ref, out, coords = refs
    mine, other = halves(place, mine_ref.shape[1])
    for cols, ref in ((mine, mine_ref), (other, other_ref)):
        if parts:
            (inverse,) = parts
            for base, inv in ((0, inverse[:, :R]), (R, inverse[:, R:])):
                coords[base : base + R, cols] = exact_dot(inv, ref[base : base + R]).astype(BF16)
        else:
            coords[:, cols] = ref[...]
    steps = out.shape[1]
    w_in = min_ref.shape[1] // steps
    w_out = mout_ref.shape[1] // steps
    part_in = jnp.dot(coords[:R], min_ref[...], preferred_element_type=F32).astype(BF16)
    part_out = jnp.dot(coords[R:], mout_ref[...], preferred_element_type=F32).astype(BF16)
    for h in range(steps):
        for g in range(GROUPS):
            rows = slice(g * ROWS, (g + 1) * ROWS)
            out[g, h, :, :w_in] = part_in[rows, h * w_in : (h + 1) * w_in]
            out[g, h, :, w_in:] = part_out[rows, h * w_out : (h + 1) * w_out]


def image_of(place, coords, layer_inputs, out_grads):
    steps = 8
    rows, d_in = layer_inputs.shape
    width = (d_in + out_grads.shape[1]) // steps
    return pl.pallas_call(
        image_kernel,
        out_shape=jax.ShapeDtypeStruct((GROUPS, steps, ROWS, width), BF16),
        in_specs=[SMEM] + [VMEM] * (len(coords) + 2),
        out_specs=VMEM,
        scratch_shapes=[pltpu.VMEM((2 * R, rows), BF16)],
        compiler_params=params(8),
        name="image",
    )(place, *coords, layer_inputs, out_grads)


def sum_kernel(parts, out):
    total = parts[0].astype(F32)
    for i in range(1, parts.shape[0]):
        total = total + parts[i].astype(F32)
    half = total.astype(BF16)
    for i in range(parts.shape[0]):
        out[i] = half


def sum_copies(parts):
    return pl.pallas_call(
        sum_kernel,
        out_shape=jax.ShapeDtypeStruct(parts.shape, parts.dtype),
        in_specs=[VMEM],
        out_specs=VMEM,
        compiler_params=params(4),
        name="sum_copies",
    )(parts)


def exact_dot(a, b):
    return jnp.dot(a, b, precision=lax.Precision.HIGHEST, preferred_element_type=F32)


def inverses(gram):
    half = gram.shape[1] // 2
    gram = jnp.concatenate([gram[:, :half], gram[:, half:]], axis=0)
    return eliminate([gram[:, :R], gram[:, R:]])


def total_kernel(near, far, raw, gram):
    raw[...] = near[: 2 * R] + far[: 2 * R]
    gram[...] = near[2 * R :] + far[2 * R :]


def total_of(near, far):
    tokens = near.shape[1]
    return pl.pallas_call(
        total_kernel,
        out_shape=tuple(jax.ShapeDtypeStruct((n, tokens), F32) for n in (2 * R, R // 2)),
        in_specs=[VMEM, VMEM],
        out_specs=(VMEM, VMEM),
        compiler_params=params(4),
        name="total",
    )(near, far)


def inverse_kernel(gram, out):
    out[:, :R], out[:, R:] = inverses(gram[...])


def inverse_of(gram):
    return pl.pallas_call(
        inverse_kernel,
        out_shape=jax.ShapeDtypeStruct((R, 2 * R), F32),
        in_specs=[VMEM],
        out_specs=VMEM,
        compiler_params=params(8),
        cost_estimate=pl.CostEstimate(flops=1 << 22, bytes_accessed=1 << 22, transcendentals=0),
        name="inverse",
    )(gram)


def last_kernel(place, near, far, own, theirs, split, feat):
    total = near[...] + far[...]
    inv_in, inv_out = inverses(total[2 * R :])
    co_in = exact_dot(inv_in, total[:R]).astype(BF16)
    co_out = exact_dot(inv_out, total[R : 2 * R]).astype(BF16)
    feat[...] = lax.dot_general(co_in, co_out, NT, preferred_element_type=F32) * (1.0 / LEN)
    rows = own.shape[0]
    own[...] = feat[pl.ds(pl.multiple_of(place[0] * rows, rows), rows)]
    theirs[...] = feat[pl.ds(pl.multiple_of((place[0] ^ 1) * rows, rows), rows)]
    split[0] = split3(inv_in)
    split[1] = split3(inv_out)


def last_of(place, near, far, count):
    block = jax.ShapeDtypeStruct((R // count, R), F32)
    return pl.pallas_call(
        last_kernel,
        out_shape=(block, block, jax.ShapeDtypeStruct((2, R, 3 * R), BF16)),
        in_specs=[SMEM, VMEM, VMEM],
        out_specs=(VMEM,) * 3,
        scratch_shapes=[pltpu.VMEM((R, R), F32)],
        compiler_params=params(8),
        name="last",
    )(place, near, far)


def features_kernel(place, own, got, out):
    rows = own.shape[0]
    own = jnp.concatenate([own[r : r + 1] for r in range(rows)], axis=1)
    got = jnp.concatenate([got[r : r + 1] for r in range(rows)], axis=1)
    even = (place[0] & 1) == 0
    out[0:1] = jnp.where(even, own, got)
    out[1:2] = jnp.where(even, got, own)


def features_of(place, own, got):
    return pl.pallas_call(
        features_kernel,
        out_shape=jax.ShapeDtypeStruct((2, own.size), F32),
        in_specs=[SMEM, VMEM, VMEM],
        out_specs=VMEM,
        compiler_params=params(4),
        name="features",
    )(place, own, got)


def basis_kernel(split, img_ref, in_hbm, out_hbm, b_in, b_out, sems):
    steps = img_ref.shape[1]
    w_in = b_in.shape[1] // steps
    w_out = b_out.shape[1] // steps
    copies = []
    for h in range(steps):
        img = jnp.concatenate([img_ref[g, h] for g in range(GROUPS)] * 3, axis=0)
        cols_in = slice(h * w_in, (h + 1) * w_in)
        cols_out = slice(h * w_out, (h + 1) * w_out)
        b_in[:, cols_in] = jnp.dot(split[0], img[:, :w_in], preferred_element_type=F32)
        b_out[:, cols_out] = jnp.dot(split[1], img[:, w_in:], preferred_element_type=F32)
        for n, (src, dst, cols) in enumerate([(b_in, in_hbm, cols_in), (b_out, out_hbm, cols_out)]):
            copy = pltpu.make_async_copy(src.at[:, cols], dst.at[:, cols], sems.at[h, n])
            copy.start()
            copies.append(copy)
    for copy in copies:
        copy.wait()


def basis_of(split, image, d_in, d_out):
    shapes = ((R, d_in), (R, d_out))
    return pl.pallas_call(
        basis_kernel,
        out_shape=tuple(jax.ShapeDtypeStruct(s, F32) for s in shapes),
        in_specs=[VMEM, VMEM],
        out_specs=(HBM, HBM),
        scratch_shapes=[pltpu.VMEM(s, F32) for s in shapes]
        + [pltpu.SemaphoreType.DMA((image.shape[1], 2))],
        compiler_params=params(8),
        name="basis",
    )(split, image)


CORE_SWAP = [(0, 1), (1, 0), (2, 3), (3, 2)]
CHIP_SWAP = [(0, 2), (2, 0), (1, 3), (3, 1)]


def shards(layer_inputs, out_grads, loss_mask, start_in, start_out):
    place = lax.axis_index("mp").reshape(1)
    mask = loss_mask.reshape(1, -1)
    d_in, d_out = layer_inputs.shape[1], out_grads.shape[1]

    def exchange(send, keep):
        near = add(keep, lax.ppermute(send, "mp", CORE_SWAP))
        return near, lax.ppermute(near, "mp", CHIP_SWAP)

    send, keep, layer_inputs, out_grads, mask = raw_first(
        place, start_in, start_out, layer_inputs, out_grads, mask
    )
    near, far = exchange(send, keep)
    mine = add(near, far, BF16)
    coords = (mine, lax.ppermute(mine, "mp", CORE_SWAP))
    for step in range(ITERS):
        parts = image_of(place, coords, layer_inputs, out_grads)
        grid = parts.shape
        parts = parts.reshape(grid[0] * grid[1], grid[2], grid[3])
        parts = lax.all_to_all(parts, "dp", 0, 0)
        image = lax.all_to_all(sum_copies(parts), "dp", 0, 0).reshape(grid)
        send, keep = raw_next(place, image, layer_inputs, out_grads, mask)
        near, far = exchange(send, keep)
        if step + 1 < ITERS:
            raw, gram = total_of(near, far)
            other = lax.ppermute(raw, "mp", CORE_SWAP)
            coords = (inverse_of(gram), raw, other)
    own, theirs, split = last_of(place, near, far, lax.axis_size("mp"))
    got = lax.ppermute(theirs, "mp", CORE_SWAP)
    basis_in, basis_out = basis_of(split, image, d_in, d_out)
    return (features_of(place, own, got), basis_in, basis_out)


def solution(mesh):
    in_specs = (P("dp", "mp"), P("dp", "mp"), P("dp"), P(None, "mp"), P(None, "mp"))
    out_specs = (P("dp", "mp"), P(None, "mp"), P(None, "mp"))
    return jax.shard_map(shards, mesh=mesh, in_specs=in_specs, out_specs=out_specs, check_vma=False)
```

```python
import functools

import jax
import jax.numpy as jnp
from jax import lax
from jax.experimental import pallas as pl
from jax.experimental.pallas import tpu as pltpu
from jax.sharding import PartitionSpec as P

ITERS = 2
LEN = 256
R = 64
ROWS = 16
GROUPS = R // ROWS
NT = (((1,), (1,)), ((), ()))
F32 = jnp.float32
BF16 = jnp.bfloat16


def split3(x):
    a = x.astype(BF16)
    rest = x - a.astype(F32)
    b = rest.astype(BF16)
    c = (rest - b.astype(F32)).astype(BF16)
    return jnp.concatenate([a, b, c], axis=1)


PIVOTS = 8
STAGGER_NS = 8500


def eliminate(grams, size=PIVOTS):
    n = grams[0].shape[0]
    col_id = lax.broadcasted_iota(jnp.int32, (n, n), 1)
    row_id = lax.broadcasted_iota(jnp.int32, (n, n), 0)
    eye = (col_id == row_id).astype(F32)
    sub = lax.broadcasted_iota(jnp.int32, (8, 1), 0)
    works = []
    for gram in grams:
        work = jnp.concatenate([gram, eye], axis=1)
        works.append([work[8 * i : 8 * i + 8] for i in range(n // 8)])
    for k in range(0, n, size):
        t, r = divmod(k, 8)
        for tiles in works:
            rows = [tiles[t][r + i : r + i + 1] for i in range(size)]
            wide = rows[0].shape
            p = {
                (i, j): jnp.broadcast_to(rows[i][:, k + j : k + j + 1], wide)
                for i in range(size)
                for j in range(i, size)
            }
            inv, low = [], {}
            for i in range(size):
                inv.append(1.0 / p[i, i])
                for j in range(i + 1, size):
                    low[j, i] = p[i, j] * inv[i]
                for j in range(i + 1, size):
                    for m in range(j, size):
                        p[j, m] = p[j, m] - low[j, i] * p[i, m]
                    rows[j] = rows[j] - low[j, i] * rows[i]
            s = [None] * size
            for i in reversed(range(size)):
                s[i] = rows[i] * inv[i]
                for j in range(i + 1, size):
                    s[i] = s[i] - low[j, i] * s[j]
            for i in range(t, n // 8):
                tile = tiles[i]
                if i == t:
                    new = tile
                    if r + size < 8:
                        for j in range(size):
                            col = jnp.where(sub >= r + size, tile[:, k + j : k + j + 1], 0.0)
                            new = new - col * s[j]
                    for j in range(1, size):
                        new = jnp.where(sub == r + j, rows[j], new)
                    tiles[i] = new
                else:
                    new = tile
                    for j in range(size):
                        new = new - tile[:, k + j : k + j + 1] * s[j]
                    tiles[i] = new
    out = []
    for tiles in works:
        work = jnp.concatenate(tiles, axis=0)
        diag = jnp.sum(jnp.where(col_id == row_id, work[:, :n], 0.0), axis=1, keepdims=True)
        out.append(work[:, n:] * (1.0 / jnp.sqrt(diag)))
    return out


def params(mib):
    return pltpu.CompilerParams(vmem_limit_bytes=mib << 20)


VMEM = pl.BlockSpec(memory_space=pltpu.VMEM)
SMEM = pl.BlockSpec(memory_space=pltpu.SMEM)
HBM = pl.BlockSpec(memory_space=pltpu.HBM)


def halves(place, tokens):
    core = place[0] & 1
    mine = pl.ds(pl.multiple_of(core * tokens, tokens), tokens)
    other = pl.ds(pl.multiple_of((1 - core) * tokens, tokens), tokens)
    return mine, other


def first_kernel(place, bin_hbm, bout_hbm, min_hbm, mout_hbm, mask_hbm, *refs):
    send, keep, mins, mouts, mask, bins, bouts, ints, acc, sems, mask_sem = refs
    steps = sems.shape[0]
    pairs = ((bin_hbm, bins), (min_hbm, mins), (bout_hbm, bouts), (mout_hbm, mouts))

    def columns(ref, h):
        width = ref.shape[1] // steps
        return slice(h * width, (h + 1) * width)

    copies = []
    for h in range(steps):
        for n, (src, dst) in enumerate(pairs):
            cols = columns(dst, h)
            copy = pltpu.make_async_copy(src.at[:, cols], dst.at[:, cols], sems.at[h, n])
            copy.start()
            copies.append(copy)
    mask_copy = pltpu.make_async_copy(mask_hbm, ints, mask_sem)
    mask_copy.start()
    for h in range(steps):
        for n, (base, basis, data) in enumerate([(0, bins, mins), (R, bouts, mouts)]):
            copies[4 * h + 2 * n].wait()
            copies[4 * h + 2 * n + 1].wait()
            cols = columns(basis, h)
            half = (basis[:, cols].astype(F32) * (1.0 / 128.0)).astype(BF16)
            part = lax.dot_general(half, data[:, cols], NT, preferred_element_type=F32)
            if h == 0:
                acc[base : base + R] = part
            else:
                acc[base : base + R] += part
    mask_copy.wait()
    mask[...] = ints[...].astype(F32)
    acc[R:] = acc[R:] * mask[...]
    mine, other = halves(place, acc.shape[1] // 2)
    keep[...] = acc[:, mine]
    send[...] = acc[:, other]


def raw_first(place, *whole):
    start_in, start_out, layer_inputs, out_grads, mask = whole
    rows = layer_inputs.shape[0]
    shape = jax.ShapeDtypeStruct((2 * R, rows // 2), F32)
    return pl.pallas_call(
        first_kernel,
        out_shape=(
            shape,
            shape,
            jax.ShapeDtypeStruct(layer_inputs.shape, BF16),
            jax.ShapeDtypeStruct(out_grads.shape, BF16),
            jax.ShapeDtypeStruct(mask.shape, F32),
        ),
        in_specs=[SMEM, HBM, HBM, HBM, HBM, HBM],
        out_specs=(VMEM,) * 5,
        scratch_shapes=[
            pltpu.VMEM(start_in.shape, jnp.int32),
            pltpu.VMEM(start_out.shape, jnp.int32),
            pltpu.VMEM(mask.shape, jnp.int32),
            pltpu.VMEM((2 * R, rows), F32),
            pltpu.SemaphoreType.DMA((8, 4)),
            pltpu.SemaphoreType.DMA,
        ],
        compiler_params=params(8),
        name="raw_first",
    )(place, *(pltpu.with_memory_space_constraint(x, pltpu.HBM) for x in whole))


def half_coords(tokens, img_in, img_out, min_ref, mout_ref, mask, out):
    part = lax.dot_general(img_in, min_ref[tokens, :], NT, preferred_element_type=F32)
    out[:R] = part
    part = lax.dot_general(img_out, mout_ref[tokens, :], NT, preferred_element_type=F32)
    out[R : 2 * R] = part * mask[:, tokens]


def send_kernel(place, img_ref, min_ref, mout_ref, mask, send, img_in, img_out):
    steps = img_ref.shape[1]
    w_in = img_in.shape[1] // steps
    w_out = img_out.shape[1] // steps
    for h in range(steps):
        for g in range(GROUPS):
            rows = slice(g * ROWS, (g + 1) * ROWS)
            img_in[rows, h * w_in : (h + 1) * w_in] = img_ref[g, h, :, :w_in]
            img_out[rows, h * w_out : (h + 1) * w_out] = img_ref[g, h, :, w_in:]
    half_in, half_out = img_in[...], img_out[...]
    _, other = halves(place, send.shape[1])
    half_coords(other, half_in, half_out, min_ref, mout_ref, mask, send)
    gram_in = lax.dot_general(half_in, half_in, NT, preferred_element_type=F32)
    gram_out = lax.dot_general(half_out, half_out, NT, preferred_element_type=F32)
    gram = jnp.concatenate([gram_in, gram_out], axis=1)
    send[2 * R :] = jnp.concatenate([gram[: R // 2], gram[R // 2 :]], axis=1)


def raw_send(place, image, layer_inputs, out_grads, mask):
    rows, d_in = layer_inputs.shape
    d_out = out_grads.shape[1]
    return pl.pallas_call(
        send_kernel,
        out_shape=(
            jax.ShapeDtypeStruct((2 * R + R // 2, rows // 2), F32),
            jax.ShapeDtypeStruct((R, d_in), BF16),
            jax.ShapeDtypeStruct((R, d_out), BF16),
        ),
        in_specs=[SMEM, VMEM, VMEM, VMEM, VMEM],
        out_specs=(VMEM,) * 3,
        compiler_params=params(8),
        name="raw_send",
    )(place, image, layer_inputs, out_grads, mask)


def keep_kernel(place, img_in, img_out, min_ref, mout_ref, mask, keep):
    mine, _ = halves(place, keep.shape[1])
    half_coords(mine, img_in[...], img_out[...], min_ref, mout_ref, mask, keep)


def raw_keep(place, img_in, img_out, layer_inputs, out_grads, mask):
    rows = layer_inputs.shape[0]
    return pl.pallas_call(
        keep_kernel,
        out_shape=jax.ShapeDtypeStruct((2 * R, rows // 2), F32),
        in_specs=[SMEM] + [VMEM] * 5,
        out_specs=VMEM,
        compiler_params=params(8),
        cost_estimate=pl.CostEstimate(flops=1 << 29, bytes_accessed=1 << 22, transcendentals=0),
        name="raw_keep",
    )(place, img_in, img_out, layer_inputs, out_grads, mask)


def near_kernel(keep, send, got, out):
    top = keep.shape[0]
    out[:top] = keep[...] + got[:top]
    out[top:] = send[top:] + got[top:]


def near_of(keep, send, got):
    return pl.pallas_call(
        near_kernel,
        out_shape=jax.ShapeDtypeStruct(send.shape, F32),
        in_specs=[VMEM] * 3,
        out_specs=VMEM,
        compiler_params=params(4),
        name="near",
    )(keep, send, got)


def add_kernel(a, b, out):
    out[...] = (a[...] + b[...]).astype(out.dtype)


def add(a, b, dtype=F32):
    return pl.pallas_call(
        add_kernel,
        out_shape=jax.ShapeDtypeStruct(a.shape, dtype),
        in_specs=[VMEM, VMEM],
        out_specs=VMEM,
        compiler_params=params(4),
        name="add",
    )(a, b)


def image_kernel(place, *refs):
    *parts, mine_ref, other_ref, min_ref, mout_ref, out, coords = refs
    mine, other = halves(place, mine_ref.shape[1])

    @pl.when((place[0] & 1) == 1)
    def _():
        pl.delay(STAGGER_NS)

    for cols, ref in ((mine, mine_ref), (other, other_ref)):
        if parts:
            (inverse,) = parts
            for base, inv in ((0, inverse[:, :R]), (R, inverse[:, R:])):
                coords[base : base + R, cols] = exact_dot(inv, ref[base : base + R]).astype(BF16)
        else:
            coords[:, cols] = ref[...]
    steps = out.shape[1]
    w_in = min_ref.shape[1] // steps
    w_out = mout_ref.shape[1] // steps
    part_in = jnp.dot(coords[:R], min_ref[...], preferred_element_type=F32).astype(BF16)
    part_out = jnp.dot(coords[R:], mout_ref[...], preferred_element_type=F32).astype(BF16)
    for h in range(steps):
        for g in range(GROUPS):
            rows = slice(g * ROWS, (g + 1) * ROWS)
            out[g, h, :, :w_in] = part_in[rows, h * w_in : (h + 1) * w_in]
            out[g, h, :, w_in:] = part_out[rows, h * w_out : (h + 1) * w_out]


def image_of(place, coords, layer_inputs, out_grads):
    steps = 8
    rows, d_in = layer_inputs.shape
    width = (d_in + out_grads.shape[1]) // steps
    return pl.pallas_call(
        image_kernel,
        out_shape=jax.ShapeDtypeStruct((GROUPS, steps, ROWS, width), BF16),
        in_specs=[SMEM] + [VMEM] * (len(coords) + 2),
        out_specs=VMEM,
        scratch_shapes=[pltpu.VMEM((2 * R, rows), BF16)],
        compiler_params=params(8),
        name="image",
    )(place, *coords, layer_inputs, out_grads)


def sum_kernel(parts, out):
    total = parts[0].astype(F32)
    for i in range(1, parts.shape[0]):
        total = total + parts[i].astype(F32)
    half = total.astype(BF16)
    for i in range(parts.shape[0]):
        out[i] = half


def sum_copies(parts):
    return pl.pallas_call(
        sum_kernel,
        out_shape=jax.ShapeDtypeStruct(parts.shape, parts.dtype),
        in_specs=[VMEM],
        out_specs=VMEM,
        compiler_params=params(4),
        name="sum_copies",
    )(parts)


def exact_dot(a, b):
    return jnp.dot(a, b, precision=lax.Precision.HIGHEST, preferred_element_type=F32)


def inverses(gram):
    half = gram.shape[1] // 2
    gram = jnp.concatenate([gram[:, :half], gram[:, half:]], axis=0)
    return eliminate([gram[:, :R], gram[:, R:]])


def total_kernel(near, far, raw, gram):
    raw[...] = near[: 2 * R] + far[: 2 * R]
    gram[...] = near[2 * R :] + far[2 * R :]


def total_of(near, far):
    tokens = near.shape[1]
    return pl.pallas_call(
        total_kernel,
        out_shape=tuple(jax.ShapeDtypeStruct((n, tokens), F32) for n in (2 * R, R // 2)),
        in_specs=[VMEM, VMEM],
        out_specs=(VMEM, VMEM),
        compiler_params=params(4),
        name="total",
    )(near, far)


def inverse_kernel(gram, out):
    out[:, :R], out[:, R:] = inverses(gram[...])


def inverse_of(gram):
    return pl.pallas_call(
        inverse_kernel,
        out_shape=jax.ShapeDtypeStruct((R, 2 * R), F32),
        in_specs=[VMEM],
        out_specs=VMEM,
        compiler_params=params(8),
        cost_estimate=pl.CostEstimate(flops=1 << 22, bytes_accessed=1 << 22, transcendentals=0),
        name="inverse",
    )(gram)


def last_kernel(place, near, far, own, theirs, split, feat):
    total = near[...] + far[...]
    inv_in, inv_out = inverses(total[2 * R :])
    co_in = exact_dot(inv_in, total[:R]).astype(BF16)
    co_out = exact_dot(inv_out, total[R : 2 * R]).astype(BF16)
    feat[...] = lax.dot_general(co_in, co_out, NT, preferred_element_type=F32) * (1.0 / LEN)
    rows = own.shape[0]
    own[...] = feat[pl.ds(pl.multiple_of(place[0] * rows, rows), rows)]
    theirs[...] = feat[pl.ds(pl.multiple_of((place[0] ^ 1) * rows, rows), rows)]
    split[0] = split3(inv_in)
    split[1] = split3(inv_out)


def last_of(place, near, far, count):
    block = jax.ShapeDtypeStruct((R // count, R), F32)
    return pl.pallas_call(
        last_kernel,
        out_shape=(block, block, jax.ShapeDtypeStruct((2, R, 3 * R), BF16)),
        in_specs=[SMEM, VMEM, VMEM],
        out_specs=(VMEM,) * 3,
        scratch_shapes=[pltpu.VMEM((R, R), F32)],
        compiler_params=params(8),
        name="last",
    )(place, near, far)


def features_kernel(place, own, got, out):
    rows = own.shape[0]
    own = jnp.concatenate([own[r : r + 1] for r in range(rows)], axis=1)
    got = jnp.concatenate([got[r : r + 1] for r in range(rows)], axis=1)
    even = (place[0] & 1) == 0
    out[0:1] = jnp.where(even, own, got)
    out[1:2] = jnp.where(even, got, own)


def features_of(place, own, got):
    return pl.pallas_call(
        features_kernel,
        out_shape=jax.ShapeDtypeStruct((2, own.size), F32),
        in_specs=[SMEM, VMEM, VMEM],
        out_specs=VMEM,
        compiler_params=params(4),
        name="features",
    )(place, own, got)


def basis_kernel(split, img_in, img_out, in_hbm, out_hbm, b_in, b_out, sems):
    steps = sems.shape[0]
    copies = []
    for h in range(steps):
        for n, (img, own, whole) in enumerate([(img_in, b_in, in_hbm), (img_out, b_out, out_hbm)]):
            width = own.shape[1] // steps
            cols = slice(h * width, (h + 1) * width)
            part = jnp.concatenate([img[:, cols]] * 3, axis=0)
            own[:, cols] = jnp.dot(split[n], part, preferred_element_type=F32)
            copy = pltpu.make_async_copy(own.at[:, cols], whole.at[:, cols], sems.at[h, n])
            copy.start()
            copies.append(copy)
    for copy in copies:
        copy.wait()


def basis_of(split, img_in, img_out):
    shapes = (img_in.shape, img_out.shape)
    return pl.pallas_call(
        basis_kernel,
        out_shape=tuple(jax.ShapeDtypeStruct(s, F32) for s in shapes),
        in_specs=[VMEM] * 3,
        out_specs=(HBM, HBM),
        scratch_shapes=[pltpu.VMEM(s, F32) for s in shapes] + [pltpu.SemaphoreType.DMA((4, 2))],
        compiler_params=params(8),
        name="basis",
    )(split, img_in, img_out)


CORE_SWAP = [(0, 1), (1, 0), (2, 3), (3, 2)]
CHIP_SWAP = [(0, 2), (2, 0), (1, 3), (3, 1)]


def shards(layer_inputs, out_grads, loss_mask, start_in, start_out):
    place = lax.axis_index("mp").reshape(1)
    mask = loss_mask.reshape(1, -1)
    send, keep, layer_inputs, out_grads, mask = raw_first(
        place, start_in, start_out, layer_inputs, out_grads, mask
    )
    near = add(keep, lax.ppermute(send, "mp", CORE_SWAP))
    far = lax.ppermute(near, "mp", CHIP_SWAP)
    mine = add(near, far, BF16)
    coords = (mine, lax.ppermute(mine, "mp", CORE_SWAP))
    for step in range(ITERS):
        parts = image_of(place, coords, layer_inputs, out_grads)
        grid = parts.shape
        parts = parts.reshape(grid[0] * grid[1], grid[2], grid[3])
        parts = lax.all_to_all(parts, "dp", 0, 0)
        image = lax.all_to_all(sum_copies(parts), "dp", 0, 0).reshape(grid)
        send, img_in, img_out = raw_send(place, image, layer_inputs, out_grads, mask)
        got = lax.ppermute(send, "mp", CORE_SWAP)
        keep = raw_keep(place, img_in, img_out, layer_inputs, out_grads, mask)
        near = near_of(keep, send, got)
        far = lax.ppermute(near, "mp", CHIP_SWAP)
        if step + 1 < ITERS:
            raw, gram = total_of(near, far)
            other = lax.ppermute(raw, "mp", CORE_SWAP)
            coords = (inverse_of(gram), raw, other)
    own, theirs, split = last_of(place, near, far, lax.axis_size("mp"))
    got = lax.ppermute(theirs, "mp", CORE_SWAP)
    basis_in, basis_out = basis_of(split, img_in, img_out)
    return (features_of(place, own, got), basis_in, basis_out)


def solution(mesh):
    in_specs = (P("dp", "mp"), P("dp", "mp"), P("dp"), P(None, "mp"), P(None, "mp"))
    out_specs = (P("dp", "mp"), P(None, "mp"), P(None, "mp"))
    return jax.shard_map(shards, mesh=mesh, in_specs=in_specs, out_specs=out_specs, check_vma=False)
```

```python
import functools

import jax
import jax.numpy as jnp
from jax import lax
from jax.experimental import pallas as pl
from jax.experimental.pallas import tpu as pltpu
from jax.sharding import PartitionSpec as P

ITERS = 2
LEN = 256
R = 64
ROWS = 16
GROUPS = R // ROWS
NT = (((1,), (1,)), ((), ()))
F32 = jnp.float32
BF16 = jnp.bfloat16


def split3(x, axis):
    a = x.astype(BF16)
    rest = x - a.astype(F32)
    b = rest.astype(BF16)
    c = (rest - b.astype(F32)).astype(BF16)
    return jnp.concatenate([a, b, c], axis=axis)


PIVOTS = 8
STAGGER_NS = 8500


def eliminate(grams, size=PIVOTS):
    n = grams[0].shape[0]
    col_id = lax.broadcasted_iota(jnp.int32, (n, n), 1)
    row_id = lax.broadcasted_iota(jnp.int32, (n, n), 0)
    eye = (col_id == row_id).astype(F32)
    sub = lax.broadcasted_iota(jnp.int32, (8, 1), 0)
    works = []
    for gram in grams:
        work = jnp.concatenate([gram, eye], axis=1)
        works.append([work[8 * i : 8 * i + 8] for i in range(n // 8)])
    for k in range(0, n, size):
        t, r = divmod(k, 8)
        for tiles in works:
            rows = [tiles[t][r + i : r + i + 1] for i in range(size)]
            wide = rows[0].shape
            p = {
                (i, j): jnp.broadcast_to(rows[i][:, k + j : k + j + 1], wide)
                for i in range(size)
                for j in range(i, size)
            }
            inv, low = [], {}
            for i in range(size):
                inv.append(1.0 / p[i, i])
                for j in range(i + 1, size):
                    low[j, i] = p[i, j] * inv[i]
                for j in range(i + 1, size):
                    for m in range(j, size):
                        p[j, m] = p[j, m] - low[j, i] * p[i, m]
                    rows[j] = rows[j] - low[j, i] * rows[i]
            s = [None] * size
            for i in reversed(range(size)):
                s[i] = rows[i] * inv[i]
                for j in range(i + 1, size):
                    s[i] = s[i] - low[j, i] * s[j]
            for i in range(t, n // 8):
                tile = tiles[i]
                if i == t:
                    new = tile
                    if r + size < 8:
                        for j in range(size):
                            col = jnp.where(sub >= r + size, tile[:, k + j : k + j + 1], 0.0)
                            new = new - col * s[j]
                    for j in range(1, size):
                        new = jnp.where(sub == r + j, rows[j], new)
                    tiles[i] = new
                else:
                    new = tile
                    for j in range(size):
                        new = new - tile[:, k + j : k + j + 1] * s[j]
                    tiles[i] = new
    out = []
    for tiles in works:
        work = jnp.concatenate(tiles, axis=0)
        diag = jnp.sum(jnp.where(col_id == row_id, work[:, :n], 0.0), axis=1, keepdims=True)
        out.append(work[:, n:] * (1.0 / jnp.sqrt(diag)))
    return out


def params(mib):
    return pltpu.CompilerParams(vmem_limit_bytes=mib << 20)


VMEM = pl.BlockSpec(memory_space=pltpu.VMEM)
SMEM = pl.BlockSpec(memory_space=pltpu.SMEM)
HBM = pl.BlockSpec(memory_space=pltpu.HBM)


def halves(place, tokens):
    core = place[0] & 1
    mine = pl.ds(pl.multiple_of(core * tokens, tokens), tokens)
    other = pl.ds(pl.multiple_of((1 - core) * tokens, tokens), tokens)
    return mine, other


def first_kernel(place, bin_hbm, bout_hbm, min_hbm, mout_hbm, mask_hbm, *refs):
    send, keep, mins, mouts, mask, bins, bouts, ints, acc, sems, mask_sem = refs
    steps = sems.shape[0]
    pairs = ((bin_hbm, bins), (min_hbm, mins), (bout_hbm, bouts), (mout_hbm, mouts))

    def columns(ref, h):
        width = ref.shape[1] // steps
        return slice(h * width, (h + 1) * width)

    copies = []
    for h in range(steps):
        for n, (src, dst) in enumerate(pairs):
            cols = columns(dst, h)
            copy = pltpu.make_async_copy(src.at[:, cols], dst.at[:, cols], sems.at[h, n])
            copy.start()
            copies.append(copy)
    mask_copy = pltpu.make_async_copy(mask_hbm, ints, mask_sem)
    mask_copy.start()
    for h in range(steps):
        for n, (base, basis, data) in enumerate([(0, bins, mins), (R, bouts, mouts)]):
            copies[4 * h + 2 * n].wait()
            copies[4 * h + 2 * n + 1].wait()
            cols = columns(basis, h)
            half = (basis[:, cols].astype(F32) * (1.0 / 128.0)).astype(BF16)
            part = lax.dot_general(half, data[:, cols], NT, preferred_element_type=F32)
            if h == 0:
                acc[base : base + R] = part
            else:
                acc[base : base + R] += part
    mask_copy.wait()
    mask[...] = ints[...].astype(F32)
    acc[R:] = acc[R:] * mask[...]
    mine, other = halves(place, acc.shape[1] // 2)
    keep[...] = acc[:, mine]
    send[...] = acc[:, other]


def raw_first(place, *whole):
    start_in, start_out, layer_inputs, out_grads, mask = whole
    rows = layer_inputs.shape[0]
    shape = jax.ShapeDtypeStruct((2 * R, rows // 2), F32)
    return pl.pallas_call(
        first_kernel,
        out_shape=(
            shape,
            shape,
            jax.ShapeDtypeStruct(layer_inputs.shape, BF16),
            jax.ShapeDtypeStruct(out_grads.shape, BF16),
            jax.ShapeDtypeStruct(mask.shape, F32),
        ),
        in_specs=[SMEM, HBM, HBM, HBM, HBM, HBM],
        out_specs=(VMEM,) * 5,
        scratch_shapes=[
            pltpu.VMEM(start_in.shape, jnp.int32),
            pltpu.VMEM(start_out.shape, jnp.int32),
            pltpu.VMEM(mask.shape, jnp.int32),
            pltpu.VMEM((2 * R, rows), F32),
            pltpu.SemaphoreType.DMA((8, 4)),
            pltpu.SemaphoreType.DMA,
        ],
        compiler_params=params(8),
        name="raw_first",
    )(place, *(pltpu.with_memory_space_constraint(x, pltpu.HBM) for x in whole))


def half_coords(tokens, img_in, img_out, min_ref, mout_ref, mask, out):
    part = lax.dot_general(img_in, min_ref[tokens, :], NT, preferred_element_type=F32)
    out[:R] = part
    part = lax.dot_general(img_out, mout_ref[tokens, :], NT, preferred_element_type=F32)
    out[R : 2 * R] = part * mask[:, tokens]


def send_kernel(place, img_ref, min_ref, mout_ref, mask, send, img_in, img_out):
    steps = img_ref.shape[1]
    w_in = img_in.shape[1] // steps
    w_out = img_out.shape[1] // steps
    for h in range(steps):
        for g in range(GROUPS):
            rows = slice(g * ROWS, (g + 1) * ROWS)
            img_in[rows, h * w_in : (h + 1) * w_in] = img_ref[g, h, :, :w_in]
            img_out[rows, h * w_out : (h + 1) * w_out] = img_ref[g, h, :, w_in:]
    half_in, half_out = img_in[...], img_out[...]
    _, other = halves(place, send.shape[1])
    half_coords(other, half_in, half_out, min_ref, mout_ref, mask, send)
    gram_in = lax.dot_general(half_in, half_in, NT, preferred_element_type=F32)
    gram_out = lax.dot_general(half_out, half_out, NT, preferred_element_type=F32)
    gram = jnp.concatenate([gram_in, gram_out], axis=1)
    send[2 * R :] = jnp.concatenate([gram[: R // 2], gram[R // 2 :]], axis=1)


def raw_send(place, image, layer_inputs, out_grads, mask):
    rows, d_in = layer_inputs.shape
    d_out = out_grads.shape[1]
    return pl.pallas_call(
        send_kernel,
        out_shape=(
            jax.ShapeDtypeStruct((2 * R + R // 2, rows // 2), F32),
            jax.ShapeDtypeStruct((R, d_in), BF16),
            jax.ShapeDtypeStruct((R, d_out), BF16),
        ),
        in_specs=[SMEM, VMEM, VMEM, VMEM, VMEM],
        out_specs=(VMEM,) * 3,
        compiler_params=params(8),
        name="raw_send",
    )(place, image, layer_inputs, out_grads, mask)


def keep_kernel(place, img_in, img_out, min_ref, mout_ref, mask, keep):
    mine, _ = halves(place, keep.shape[1])
    half_coords(mine, img_in[...], img_out[...], min_ref, mout_ref, mask, keep)


def raw_keep(place, img_in, img_out, layer_inputs, out_grads, mask):
    rows = layer_inputs.shape[0]
    return pl.pallas_call(
        keep_kernel,
        out_shape=jax.ShapeDtypeStruct((2 * R, rows // 2), F32),
        in_specs=[SMEM] + [VMEM] * 5,
        out_specs=VMEM,
        compiler_params=params(8),
        cost_estimate=pl.CostEstimate(flops=1 << 29, bytes_accessed=1 << 22, transcendentals=0),
        name="raw_keep",
    )(place, img_in, img_out, layer_inputs, out_grads, mask)


def near_kernel(keep, *refs):
    *sent, got, near, out = refs
    top = keep.shape[0]
    near[:top] = keep[...] + got[:top]
    out[:top] = near[:top].astype(BF16)
    if sent:
        near[top:] = sent[0][top:] + got[top:]
        out[top:] = split3(near[top:], 0)


def near_of(keep, sent, got):
    top, tokens = keep.shape
    grams = got.shape[0] - top
    return pl.pallas_call(
        near_kernel,
        out_shape=(
            jax.ShapeDtypeStruct(got.shape, F32),
            jax.ShapeDtypeStruct((top + 3 * grams, tokens), BF16),
        ),
        in_specs=[VMEM] * (3 if grams else 2),
        out_specs=(VMEM, VMEM),
        compiler_params=params(4),
        name="near",
    )(keep, *([sent] if grams else []), got)


def whole_raw(near, far):
    return near[: 2 * R] + far[: 2 * R].astype(F32)


def whole_gram(near, far):
    a, b, c = (far[2 * R + i * R // 2 : 2 * R + (i + 1) * R // 2].astype(F32) for i in range(3))
    return near[2 * R :] + (a + b + c)


def coords_kernel(near, far, out):
    out[...] = whole_raw(near, far).astype(BF16)


def coords_of(near, far):
    return pl.pallas_call(
        coords_kernel,
        out_shape=jax.ShapeDtypeStruct(far.shape, BF16),
        in_specs=[VMEM, VMEM],
        out_specs=VMEM,
        compiler_params=params(4),
        name="coords",
    )(near, far)


def image_kernel(place, *refs):
    *parts, mine_ref, other_ref, min_ref, mout_ref, out, coords = refs
    mine, other = halves(place, mine_ref.shape[1])

    @pl.when((place[0] & 1) == 1)
    def _():
        pl.delay(STAGGER_NS)

    for cols, ref in ((mine, mine_ref), (other, other_ref)):
        if parts:
            (inverse,) = parts
            for base, inv in ((0, inverse[:, :R]), (R, inverse[:, R:])):
                coords[base : base + R, cols] = exact_dot(inv, ref[base : base + R]).astype(BF16)
        else:
            coords[:, cols] = ref[...]
    steps = out.shape[1]
    w_in = min_ref.shape[1] // steps
    w_out = mout_ref.shape[1] // steps
    part_in = jnp.dot(coords[:R], min_ref[...], preferred_element_type=F32).astype(BF16)
    part_out = jnp.dot(coords[R:], mout_ref[...], preferred_element_type=F32).astype(BF16)
    for h in range(steps):
        for g in range(GROUPS):
            rows = slice(g * ROWS, (g + 1) * ROWS)
            out[g, h, :, :w_in] = part_in[rows, h * w_in : (h + 1) * w_in]
            out[g, h, :, w_in:] = part_out[rows, h * w_out : (h + 1) * w_out]


def image_of(place, coords, layer_inputs, out_grads):
    steps = 8
    rows, d_in = layer_inputs.shape
    width = (d_in + out_grads.shape[1]) // steps
    return pl.pallas_call(
        image_kernel,
        out_shape=jax.ShapeDtypeStruct((GROUPS, steps, ROWS, width), BF16),
        in_specs=[SMEM] + [VMEM] * (len(coords) + 2),
        out_specs=VMEM,
        scratch_shapes=[pltpu.VMEM((2 * R, rows), BF16)],
        compiler_params=params(8),
        name="image",
    )(place, *coords, layer_inputs, out_grads)


def sum_kernel(parts, out):
    total = parts[0].astype(F32)
    for i in range(1, parts.shape[0]):
        total = total + parts[i].astype(F32)
    half = total.astype(BF16)
    for i in range(parts.shape[0]):
        out[i] = half


def sum_copies(parts):
    return pl.pallas_call(
        sum_kernel,
        out_shape=jax.ShapeDtypeStruct(parts.shape, parts.dtype),
        in_specs=[VMEM],
        out_specs=VMEM,
        compiler_params=params(4),
        name="sum_copies",
    )(parts)


def exact_dot(a, b):
    return jnp.dot(a, b, precision=lax.Precision.HIGHEST, preferred_element_type=F32)


def inverses(gram):
    half = gram.shape[1] // 2
    gram = jnp.concatenate([gram[:, :half], gram[:, half:]], axis=0)
    return eliminate([gram[:, :R], gram[:, R:]])


def total_kernel(near, far, raw, gram):
    raw[...] = whole_raw(near, far)
    gram[...] = whole_gram(near, far)


def total_of(near, far):
    tokens = near.shape[1]
    return pl.pallas_call(
        total_kernel,
        out_shape=tuple(jax.ShapeDtypeStruct((n, tokens), F32) for n in (2 * R, R // 2)),
        in_specs=[VMEM, VMEM],
        out_specs=(VMEM, VMEM),
        compiler_params=params(4),
        name="total",
    )(near, far)


def inverse_kernel(gram, out):
    out[:, :R], out[:, R:] = inverses(gram[...])


def inverse_of(gram):
    return pl.pallas_call(
        inverse_kernel,
        out_shape=jax.ShapeDtypeStruct((R, 2 * R), F32),
        in_specs=[VMEM],
        out_specs=VMEM,
        compiler_params=params(8),
        cost_estimate=pl.CostEstimate(flops=1 << 22, bytes_accessed=1 << 22, transcendentals=0),
        name="inverse",
    )(gram)


def last_kernel(place, near, far, own, theirs, split, feat):
    total = whole_raw(near, far)
    inv_in, inv_out = inverses(whole_gram(near, far))
    co_in = exact_dot(inv_in, total[:R]).astype(BF16)
    co_out = exact_dot(inv_out, total[R:]).astype(BF16)
    feat[...] = lax.dot_general(co_in, co_out, NT, preferred_element_type=F32) * (1.0 / LEN)
    rows = own.shape[0]
    own[...] = feat[pl.ds(pl.multiple_of(place[0] * rows, rows), rows)]
    theirs[...] = feat[pl.ds(pl.multiple_of((place[0] ^ 1) * rows, rows), rows)]
    split[0] = split3(inv_in, 1)
    split[1] = split3(inv_out, 1)


def last_of(place, near, far, count):
    block = jax.ShapeDtypeStruct((R // count, R), F32)
    return pl.pallas_call(
        last_kernel,
        out_shape=(block, block, jax.ShapeDtypeStruct((2, R, 3 * R), BF16)),
        in_specs=[SMEM, VMEM, VMEM],
        out_specs=(VMEM,) * 3,
        scratch_shapes=[pltpu.VMEM((R, R), F32)],
        compiler_params=params(8),
        name="last",
    )(place, near, far)


def features_kernel(place, own, got, out):
    rows = own.shape[0]
    own = jnp.concatenate([own[r : r + 1] for r in range(rows)], axis=1)
    got = jnp.concatenate([got[r : r + 1] for r in range(rows)], axis=1)
    even = (place[0] & 1) == 0
    out[0:1] = jnp.where(even, own, got)
    out[1:2] = jnp.where(even, got, own)


def features_of(place, own, got):
    return pl.pallas_call(
        features_kernel,
        out_shape=jax.ShapeDtypeStruct((2, own.size), F32),
        in_specs=[SMEM, VMEM, VMEM],
        out_specs=VMEM,
        compiler_params=params(4),
        name="features",
    )(place, own, got)


def basis_kernel(split, img_in, img_out, in_hbm, out_hbm, b_in, b_out, sems):
    steps = sems.shape[0]
    copies = []
    for h in range(steps):
        for n, (img, own, whole) in enumerate([(img_in, b_in, in_hbm), (img_out, b_out, out_hbm)]):
            width = own.shape[1] // steps
            cols = slice(h * width, (h + 1) * width)
            part = jnp.concatenate([img[:, cols]] * 3, axis=0)
            own[:, cols] = jnp.dot(split[n], part, preferred_element_type=F32)
            copy = pltpu.make_async_copy(own.at[:, cols], whole.at[:, cols], sems.at[h, n])
            copy.start()
            copies.append(copy)
    for copy in copies:
        copy.wait()


def basis_of(split, img_in, img_out):
    shapes = (img_in.shape, img_out.shape)
    return pl.pallas_call(
        basis_kernel,
        out_shape=tuple(jax.ShapeDtypeStruct(s, F32) for s in shapes),
        in_specs=[VMEM] * 3,
        out_specs=(HBM, HBM),
        scratch_shapes=[pltpu.VMEM(s, F32) for s in shapes] + [pltpu.SemaphoreType.DMA((4, 2))],
        compiler_params=params(8),
        name="basis",
    )(split, img_in, img_out)


CORE_SWAP = [(0, 1), (1, 0), (2, 3), (3, 2)]
CHIP_SWAP = [(0, 2), (2, 0), (1, 3), (3, 1)]


def shards(layer_inputs, out_grads, loss_mask, start_in, start_out):
    place = lax.axis_index("mp").reshape(1)
    mask = loss_mask.reshape(1, -1)
    send, keep, layer_inputs, out_grads, mask = raw_first(
        place, start_in, start_out, layer_inputs, out_grads, mask
    )
    near, out = near_of(keep, send, lax.ppermute(send, "mp", CORE_SWAP))
    mine = coords_of(near, lax.ppermute(out, "mp", CHIP_SWAP))
    coords = (mine, lax.ppermute(mine, "mp", CORE_SWAP))
    for step in range(ITERS):
        parts = image_of(place, coords, layer_inputs, out_grads)
        grid = parts.shape
        parts = parts.reshape(grid[0] * grid[1], grid[2], grid[3])
        parts = lax.all_to_all(parts, "dp", 0, 0)
        image = lax.all_to_all(sum_copies(parts), "dp", 0, 0).reshape(grid)
        send, img_in, img_out = raw_send(place, image, layer_inputs, out_grads, mask)
        got = lax.ppermute(send, "mp", CORE_SWAP)
        keep = raw_keep(place, img_in, img_out, layer_inputs, out_grads, mask)
        near, out = near_of(keep, send, got)
        far = lax.ppermute(out, "mp", CHIP_SWAP)
        if step + 1 < ITERS:
            raw, gram = total_of(near, far)
            other = lax.ppermute(raw, "mp", CORE_SWAP)
            coords = (inverse_of(gram), raw, other)
    own, theirs, split = last_of(place, near, far, lax.axis_size("mp"))
    got = lax.ppermute(theirs, "mp", CORE_SWAP)
    basis_in, basis_out = basis_of(split, img_in, img_out)
    return (features_of(place, own, got), basis_in, basis_out)


def solution(mesh):
    in_specs = (P("dp", "mp"), P("dp", "mp"), P("dp"), P(None, "mp"), P(None, "mp"))
    out_specs = (P("dp", "mp"), P(None, "mp"), P(None, "mp"))
    return jax.shard_map(shards, mesh=mesh, in_specs=in_specs, out_specs=out_specs, check_vma=False)
```

```python
import functools

import jax
import jax.numpy as jnp
from jax import lax
from jax.experimental import pallas as pl
from jax.experimental.pallas import tpu as pltpu
from jax.sharding import PartitionSpec as P

ITERS = 2
LEN = 256
R = 64
ROWS = 16
GROUPS = R // ROWS
NT = (((1,), (1,)), ((), ()))
F32 = jnp.float32
BF16 = jnp.bfloat16


def split3(x, axis):
    a = x.astype(BF16)
    rest = x - a.astype(F32)
    b = rest.astype(BF16)
    c = (rest - b.astype(F32)).astype(BF16)
    return jnp.concatenate([a, b, c], axis=axis)


PIVOTS = 8
STAGGER_NS = 8500


def eliminate(grams, size=PIVOTS):
    n = grams[0].shape[0]
    col_id = lax.broadcasted_iota(jnp.int32, (n, n), 1)
    row_id = lax.broadcasted_iota(jnp.int32, (n, n), 0)
    eye = (col_id == row_id).astype(F32)
    sub = lax.broadcasted_iota(jnp.int32, (8, 1), 0)
    works = []
    for gram in grams:
        work = jnp.concatenate([gram, eye], axis=1)
        works.append([work[8 * i : 8 * i + 8] for i in range(n // 8)])
    for k in range(0, n, size):
        t, r = divmod(k, 8)
        for tiles in works:
            rows = [tiles[t][r + i : r + i + 1] for i in range(size)]
            wide = rows[0].shape
            p = {
                (i, j): jnp.broadcast_to(rows[i][:, k + j : k + j + 1], wide)
                for i in range(size)
                for j in range(i, size)
            }
            inv, low = [], {}
            for i in range(size):
                inv.append(1.0 / p[i, i])
                for j in range(i + 1, size):
                    low[j, i] = p[i, j] * inv[i]
                for j in range(i + 1, size):
                    for m in range(j, size):
                        p[j, m] = p[j, m] - low[j, i] * p[i, m]
                    rows[j] = rows[j] - low[j, i] * rows[i]
            s = [None] * size
            for i in reversed(range(size)):
                s[i] = rows[i] * inv[i]
                for j in range(i + 1, size):
                    s[i] = s[i] - low[j, i] * s[j]
            for i in range(t, n // 8):
                tile = tiles[i]
                if i == t:
                    new = tile
                    if r + size < 8:
                        for j in range(size):
                            col = jnp.where(sub >= r + size, tile[:, k + j : k + j + 1], 0.0)
                            new = new - col * s[j]
                    for j in range(1, size):
                        new = jnp.where(sub == r + j, rows[j], new)
                    tiles[i] = new
                else:
                    new = tile
                    for j in range(size):
                        new = new - tile[:, k + j : k + j + 1] * s[j]
                    tiles[i] = new
    out = []
    for tiles in works:
        work = jnp.concatenate(tiles, axis=0)
        diag = jnp.sum(jnp.where(col_id == row_id, work[:, :n], 0.0), axis=1, keepdims=True)
        out.append(work[:, n:] * (1.0 / jnp.sqrt(diag)))
    return out


def params(mib):
    return pltpu.CompilerParams(vmem_limit_bytes=mib << 20)


VMEM = pl.BlockSpec(memory_space=pltpu.VMEM)
SMEM = pl.BlockSpec(memory_space=pltpu.SMEM)
HBM = pl.BlockSpec(memory_space=pltpu.HBM)


def halves(place, tokens):
    core = place[0] & 1
    mine = pl.ds(pl.multiple_of(core * tokens, tokens), tokens)
    other = pl.ds(pl.multiple_of((1 - core) * tokens, tokens), tokens)
    return mine, other


def first_kernel(place, bin_hbm, bout_hbm, min_hbm, mout_hbm, mask_hbm, *refs):
    send, keep, mins, mouts, mask, bins, bouts, ints, acc, sems, mask_sem = refs
    steps = sems.shape[0]
    pairs = ((bin_hbm, bins), (min_hbm, mins), (bout_hbm, bouts), (mout_hbm, mouts))

    def columns(ref, h):
        width = ref.shape[1] // steps
        return slice(h * width, (h + 1) * width)

    copies = []
    for h in range(steps):
        for n, (src, dst) in enumerate(pairs):
            cols = columns(dst, h)
            copy = pltpu.make_async_copy(src.at[:, cols], dst.at[:, cols], sems.at[h, n])
            copy.start()
            copies.append(copy)
    mask_copy = pltpu.make_async_copy(mask_hbm, ints, mask_sem)
    mask_copy.start()
    for h in range(steps):
        for n, (base, basis, data) in enumerate([(0, bins, mins), (R, bouts, mouts)]):
            copies[4 * h + 2 * n].wait()
            copies[4 * h + 2 * n + 1].wait()
            cols = columns(basis, h)
            half = (basis[:, cols].astype(F32) * (1.0 / 128.0)).astype(BF16)
            part = lax.dot_general(half, data[:, cols], NT, preferred_element_type=F32)
            if h == 0:
                acc[base : base + R] = part
            else:
                acc[base : base + R] += part
    mask_copy.wait()
    mask[...] = ints[...].astype(F32)
    acc[R:] = acc[R:] * mask[...]
    mine, other = halves(place, acc.shape[1] // 2)
    keep[...] = acc[:, mine]
    send[...] = acc[:, other]


def raw_first(place, *whole):
    start_in, start_out, layer_inputs, out_grads, mask = whole
    rows = layer_inputs.shape[0]
    shape = jax.ShapeDtypeStruct((2 * R, rows // 2), F32)
    return pl.pallas_call(
        first_kernel,
        out_shape=(
            shape,
            shape,
            jax.ShapeDtypeStruct(layer_inputs.shape, BF16),
            jax.ShapeDtypeStruct(out_grads.shape, BF16),
            jax.ShapeDtypeStruct(mask.shape, F32),
        ),
        in_specs=[SMEM, HBM, HBM, HBM, HBM, HBM],
        out_specs=(VMEM,) * 5,
        scratch_shapes=[
            pltpu.VMEM(start_in.shape, jnp.int32),
            pltpu.VMEM(start_out.shape, jnp.int32),
            pltpu.VMEM(mask.shape, jnp.int32),
            pltpu.VMEM((2 * R, rows), F32),
            pltpu.SemaphoreType.DMA((8, 4)),
            pltpu.SemaphoreType.DMA,
        ],
        compiler_params=params(8),
        name="raw_first",
    )(place, *(pltpu.with_memory_space_constraint(x, pltpu.HBM) for x in whole))


def half_coords(tokens, img_in, img_out, min_ref, mout_ref, mask, out):
    part = lax.dot_general(img_in, min_ref[tokens, :], NT, preferred_element_type=F32)
    out[:R] = part
    part = lax.dot_general(img_out, mout_ref[tokens, :], NT, preferred_element_type=F32)
    out[R : 2 * R] = part * mask[:, tokens]


def send_kernel(place, img_ref, min_ref, mout_ref, mask, send, img_in, img_out):
    steps = img_ref.shape[1]
    w_in = img_in.shape[1] // steps
    w_out = img_out.shape[1] // steps
    for h in range(steps):
        for g in range(GROUPS):
            rows = slice(g * ROWS, (g + 1) * ROWS)
            img_in[rows, h * w_in : (h + 1) * w_in] = img_ref[g, h, :, :w_in]
            img_out[rows, h * w_out : (h + 1) * w_out] = img_ref[g, h, :, w_in:]
    half_in, half_out = img_in[...], img_out[...]
    _, other = halves(place, send.shape[1])
    half_coords(other, half_in, half_out, min_ref, mout_ref, mask, send)
    gram_in = lax.dot_general(half_in, half_in, NT, preferred_element_type=F32)
    gram_out = lax.dot_general(half_out, half_out, NT, preferred_element_type=F32)
    gram = jnp.concatenate([gram_in, gram_out], axis=1)
    send[2 * R :] = jnp.concatenate([gram[: R // 2], gram[R // 2 :]], axis=1)


def raw_send(place, image, layer_inputs, out_grads, mask):
    rows, d_in = layer_inputs.shape
    d_out = out_grads.shape[1]
    return pl.pallas_call(
        send_kernel,
        out_shape=(
            jax.ShapeDtypeStruct((2 * R + R // 2, rows // 2), F32),
            jax.ShapeDtypeStruct((R, d_in), BF16),
            jax.ShapeDtypeStruct((R, d_out), BF16),
        ),
        in_specs=[SMEM, VMEM, VMEM, VMEM, VMEM],
        out_specs=(VMEM,) * 3,
        compiler_params=params(8),
        name="raw_send",
    )(place, image, layer_inputs, out_grads, mask)


def keep_kernel(place, img_in, img_out, min_ref, mout_ref, mask, keep):
    mine, _ = halves(place, keep.shape[1])
    half_coords(mine, img_in[...], img_out[...], min_ref, mout_ref, mask, keep)


def raw_keep(place, img_in, img_out, layer_inputs, out_grads, mask):
    rows = layer_inputs.shape[0]
    return pl.pallas_call(
        keep_kernel,
        out_shape=jax.ShapeDtypeStruct((2 * R, rows // 2), F32),
        in_specs=[SMEM] + [VMEM] * 5,
        out_specs=VMEM,
        compiler_params=params(8),
        cost_estimate=pl.CostEstimate(flops=1 << 29, bytes_accessed=1 << 22, transcendentals=0),
        name="raw_keep",
    )(place, img_in, img_out, layer_inputs, out_grads, mask)


def near_kernel(keep, *refs):
    *sent, got, near, out = refs
    top = keep.shape[0]
    near[:top] = keep[...] + got[:top]
    out[:top] = near[:top].astype(BF16)
    if sent:
        near[top:] = sent[0][top:] + got[top:]
        out[top:] = split3(near[top:], 0)


def near_of(keep, sent, got):
    top, tokens = keep.shape
    grams = got.shape[0] - top
    return pl.pallas_call(
        near_kernel,
        out_shape=(
            jax.ShapeDtypeStruct(got.shape, F32),
            jax.ShapeDtypeStruct((top + 3 * grams, tokens), BF16),
        ),
        in_specs=[VMEM] * (3 if grams else 2),
        out_specs=(VMEM, VMEM),
        compiler_params=params(4),
        name="near",
    )(keep, *([sent] if grams else []), got)


def whole_raw(near, far):
    return near[: 2 * R] + far[: 2 * R].astype(F32)


def whole_gram(near, far):
    a, b, c = (far[2 * R + i * R // 2 : 2 * R + (i + 1) * R // 2].astype(F32) for i in range(3))
    return near[2 * R :] + (a + b + c)


def coords_kernel(near, far, out):
    out[...] = whole_raw(near, far).astype(BF16)


def coords_of(near, far):
    return pl.pallas_call(
        coords_kernel,
        out_shape=jax.ShapeDtypeStruct(far.shape, BF16),
        in_specs=[VMEM, VMEM],
        out_specs=VMEM,
        compiler_params=params(4),
        name="coords",
    )(near, far)


def image_kernel(place, *refs):
    *parts, mine_ref, other_ref, min_ref, mout_ref, out, coords = refs
    mine, other = halves(place, mine_ref.shape[1])

    @pl.when((place[0] & 1) == 1)
    def _():
        pl.delay(STAGGER_NS)

    for cols, ref in ((mine, mine_ref), (other, other_ref)):
        if parts:
            (inverse,) = parts
            for base, inv in ((0, inverse[:, :R]), (R, inverse[:, R:])):
                coords[base : base + R, cols] = exact_dot(inv, ref[base : base + R]).astype(BF16)
        else:
            coords[:, cols] = ref[...]
    steps = out.shape[1]
    w_in = min_ref.shape[1] // steps
    w_out = mout_ref.shape[1] // steps
    part_in = jnp.dot(coords[:R], min_ref[...], preferred_element_type=F32).astype(BF16)
    part_out = jnp.dot(coords[R:], mout_ref[...], preferred_element_type=F32).astype(BF16)
    for h in range(steps):
        for g in range(GROUPS):
            rows = slice(g * ROWS, (g + 1) * ROWS)
            out[g, h, :, :w_in] = part_in[rows, h * w_in : (h + 1) * w_in]
            out[g, h, :, w_in:] = part_out[rows, h * w_out : (h + 1) * w_out]


def image_of(place, coords, layer_inputs, out_grads):
    steps = 8
    rows, d_in = layer_inputs.shape
    width = (d_in + out_grads.shape[1]) // steps
    return pl.pallas_call(
        image_kernel,
        out_shape=jax.ShapeDtypeStruct((GROUPS, steps, ROWS, width), BF16),
        in_specs=[SMEM] + [VMEM] * (len(coords) + 2),
        out_specs=VMEM,
        scratch_shapes=[pltpu.VMEM((2 * R, rows), BF16)],
        compiler_params=params(8),
        name="image",
    )(place, *coords, layer_inputs, out_grads)


def sum_kernel(parts, out):
    total = parts[0].astype(F32)
    for i in range(1, parts.shape[0]):
        total = total + parts[i].astype(F32)
    half = total.astype(BF16)
    for i in range(parts.shape[0]):
        out[i] = half


def sum_copies(parts):
    return pl.pallas_call(
        sum_kernel,
        out_shape=jax.ShapeDtypeStruct(parts.shape, parts.dtype),
        in_specs=[VMEM],
        out_specs=VMEM,
        compiler_params=params(4),
        name="sum_copies",
    )(parts)


def exact_dot(a, b):
    return jnp.dot(a, b, precision=lax.Precision.HIGHEST, preferred_element_type=F32)


def inverses(gram):
    half = gram.shape[1] // 2
    gram = jnp.concatenate([gram[:, :half], gram[:, half:]], axis=0)
    return eliminate([gram[:, :R], gram[:, R:]])


def total_kernel(near, far, raw, gram):
    raw[...] = whole_raw(near, far)
    gram[...] = whole_gram(near, far)


def total_of(near, far):
    tokens = near.shape[1]
    return pl.pallas_call(
        total_kernel,
        out_shape=tuple(jax.ShapeDtypeStruct((n, tokens), F32) for n in (2 * R, R // 2)),
        in_specs=[VMEM, VMEM],
        out_specs=(VMEM, VMEM),
        compiler_params=params(4),
        name="total",
    )(near, far)


def inverse_kernel(gram, out):
    out[:, :R], out[:, R:] = inverses(gram[...])


def inverse_of(gram):
    return pl.pallas_call(
        inverse_kernel,
        out_shape=jax.ShapeDtypeStruct((R, 2 * R), F32),
        in_specs=[VMEM],
        out_specs=VMEM,
        compiler_params=params(8),
        cost_estimate=pl.CostEstimate(flops=1 << 22, bytes_accessed=1 << 22, transcendentals=0),
        name="inverse",
    )(gram)


def last_kernel(place, inverse, mine, other, img_in, img_out, *refs):
    feat, in_hbm, out_hbm, b_in, b_out, sems = refs
    steps = sems.shape[0]
    copies = []
    for n, (img, own, whole) in enumerate([(img_in, b_in, in_hbm), (img_out, b_out, out_hbm)]):
        split = split3(inverse[:, n * R : (n + 1) * R], 1)
        width = own.shape[1] // steps
        for h in range(steps):
            cols = slice(h * width, (h + 1) * width)
            part = jnp.concatenate([img[:, cols]] * 3, axis=0)
            own[:, cols] = jnp.dot(split, part, preferred_element_type=F32)
            copies.append(
                pltpu.make_async_copy(own.at[:, cols], whole.at[:, cols], sems.at[h, n])
            )
            if len(copies) > 1:
                copies[-2].start()
    copies[-1].start()
    block = feat.shape[1] // R
    inv_in = inverse[pl.ds(pl.multiple_of(place[0] * block, block), block), :][:, :R]
    found = []
    for raw in (mine, other):
        proj_in = exact_dot(inv_in, raw[:R]).astype(BF16)
        proj_out = exact_dot(inverse[:, R:], raw[R:]).astype(BF16)
        one = lax.dot_general(proj_in, proj_out, NT, preferred_element_type=F32) * (1.0 / LEN)
        found.append(jnp.concatenate([one[r : r + 1] for r in range(block)], axis=1))
    even = (place[0] & 1) == 0
    feat[0:1] = jnp.where(even, found[0], found[1])
    feat[1:2] = jnp.where(even, found[1], found[0])
    for copy in copies:
        copy.wait()


def last_of(place, coords, img_in, img_out, count):
    shapes = (img_in.shape, img_out.shape)
    return pl.pallas_call(
        last_kernel,
        out_shape=tuple(jax.ShapeDtypeStruct(s, F32) for s in ((2, R // count * R), *shapes)),
        in_specs=[SMEM] + [VMEM] * 5,
        out_specs=(VMEM, HBM, HBM),
        scratch_shapes=[pltpu.VMEM(s, F32) for s in shapes] + [pltpu.SemaphoreType.DMA((4, 2))],
        compiler_params=params(8),
        name="last",
    )(place, *coords, img_in, img_out)


CORE_SWAP = [(0, 1), (1, 0), (2, 3), (3, 2)]
CHIP_SWAP = [(0, 2), (2, 0), (1, 3), (3, 1)]


def shards(layer_inputs, out_grads, loss_mask, start_in, start_out):
    place = lax.axis_index("mp").reshape(1)
    mask = loss_mask.reshape(1, -1)
    send, keep, layer_inputs, out_grads, mask = raw_first(
        place, start_in, start_out, layer_inputs, out_grads, mask
    )
    near, out = near_of(keep, send, lax.ppermute(send, "mp", CORE_SWAP))
    mine = coords_of(near, lax.ppermute(out, "mp", CHIP_SWAP))
    coords = (mine, lax.ppermute(mine, "mp", CORE_SWAP))
    for step in range(ITERS):
        parts = image_of(place, coords, layer_inputs, out_grads)
        grid = parts.shape
        parts = parts.reshape(grid[0] * grid[1], grid[2], grid[3])
        parts = lax.all_to_all(parts, "dp", 0, 0)
        image = lax.all_to_all(sum_copies(parts), "dp", 0, 0).reshape(grid)
        send, img_in, img_out = raw_send(place, image, layer_inputs, out_grads, mask)
        got = lax.ppermute(send, "mp", CORE_SWAP)
        keep = raw_keep(place, img_in, img_out, layer_inputs, out_grads, mask)
        near, out = near_of(keep, send, got)
        far = lax.ppermute(out, "mp", CHIP_SWAP)
        raw, gram = total_of(near, far)
        other = lax.ppermute(raw, "mp", CORE_SWAP)
        coords = (inverse_of(gram), raw, other)
    return last_of(place, coords, img_in, img_out, lax.axis_size("mp"))


def solution(mesh):
    in_specs = (P("dp", "mp"), P("dp", "mp"), P("dp"), P(None, "mp"), P(None, "mp"))
    out_specs = (P("dp", "mp"), P(None, "mp"), P(None, "mp"))
    return jax.shard_map(shards, mesh=mesh, in_specs=in_specs, out_specs=out_specs, check_vma=False)
```

```python
import functools

import jax
import jax.numpy as jnp
from jax import lax
from jax.experimental import pallas as pl
from jax.experimental.pallas import tpu as pltpu
from jax.sharding import PartitionSpec as P

ITERS = 2
LEN = 256
R = 64
ROWS = 16
GROUPS = R // ROWS
NT = (((1,), (1,)), ((), ()))
F32 = jnp.float32
BF16 = jnp.bfloat16


def split3(x, axis):
    a = x.astype(BF16)
    rest = x - a.astype(F32)
    b = rest.astype(BF16)
    c = (rest - b.astype(F32)).astype(BF16)
    return jnp.concatenate([a, b, c], axis=axis)


PIVOTS = 8
STAGGER_NS = 8500


def eliminate(grams, size=PIVOTS):
    n = grams[0].shape[0]
    col_id = lax.broadcasted_iota(jnp.int32, (n, n), 1)
    row_id = lax.broadcasted_iota(jnp.int32, (n, n), 0)
    eye = (col_id == row_id).astype(F32)
    sub = lax.broadcasted_iota(jnp.int32, (8, 1), 0)
    works = []
    for gram in grams:
        work = jnp.concatenate([gram, eye], axis=1)
        works.append([work[8 * i : 8 * i + 8] for i in range(n // 8)])
    for k in range(0, n, size):
        t, r = divmod(k, 8)
        for tiles in works:
            rows = [tiles[t][r + i : r + i + 1] for i in range(size)]
            wide = rows[0].shape
            p = {
                (i, j): jnp.broadcast_to(rows[i][:, k + j : k + j + 1], wide)
                for i in range(size)
                for j in range(i, size)
            }
            inv, low = [], {}
            for i in range(size):
                inv.append(1.0 / p[i, i])
                for j in range(i + 1, size):
                    low[j, i] = p[i, j] * inv[i]
                for j in range(i + 1, size):
                    for m in range(j, size):
                        p[j, m] = p[j, m] - low[j, i] * p[i, m]
                    rows[j] = rows[j] - low[j, i] * rows[i]
            s = [None] * size
            for i in reversed(range(size)):
                s[i] = rows[i] * inv[i]
                for j in range(i + 1, size):
                    s[i] = s[i] - low[j, i] * s[j]
            for i in range(t, n // 8):
                tile = tiles[i]
                if i == t:
                    new = tile
                    if r + size < 8:
                        for j in range(size):
                            col = jnp.where(sub >= r + size, tile[:, k + j : k + j + 1], 0.0)
                            new = new - col * s[j]
                    for j in range(1, size):
                        new = jnp.where(sub == r + j, rows[j], new)
                    tiles[i] = new
                else:
                    new = tile
                    for j in range(size):
                        new = new - tile[:, k + j : k + j + 1] * s[j]
                    tiles[i] = new
    out = []
    for tiles in works:
        work = jnp.concatenate(tiles, axis=0)
        diag = jnp.sum(jnp.where(col_id == row_id, work[:, :n], 0.0), axis=1, keepdims=True)
        out.append(work[:, n:] * (1.0 / jnp.sqrt(diag)))
    return out


def params(mib):
    return pltpu.CompilerParams(vmem_limit_bytes=mib << 20)


VMEM = pl.BlockSpec(memory_space=pltpu.VMEM)
SMEM = pl.BlockSpec(memory_space=pltpu.SMEM)
HBM = pl.BlockSpec(memory_space=pltpu.HBM)


def halves(place, tokens):
    core = place[0] & 1
    mine = pl.ds(pl.multiple_of(core * tokens, tokens), tokens)
    other = pl.ds(pl.multiple_of((1 - core) * tokens, tokens), tokens)
    return mine, other


def first_kernel(place, bin_hbm, bout_hbm, min_hbm, mout_hbm, mask_hbm, *refs):
    send, keep, mins, mouts, mask, bins, bouts, ints, acc, sems, mask_sem = refs
    steps = sems.shape[0]
    pairs = ((bin_hbm, bins), (min_hbm, mins), (bout_hbm, bouts), (mout_hbm, mouts))

    def columns(ref, h):
        width = ref.shape[1] // steps
        return slice(h * width, (h + 1) * width)

    copies = []
    for h in range(steps):
        for n, (src, dst) in enumerate(pairs):
            cols = columns(dst, h)
            copy = pltpu.make_async_copy(src.at[:, cols], dst.at[:, cols], sems.at[h, n])
            copy.start()
            copies.append(copy)
    mask_copy = pltpu.make_async_copy(mask_hbm, ints, mask_sem)
    mask_copy.start()
    for h in range(steps):
        for n, (base, basis, data) in enumerate([(0, bins, mins), (R, bouts, mouts)]):
            copies[4 * h + 2 * n].wait()
            copies[4 * h + 2 * n + 1].wait()
            cols = columns(basis, h)
            half = (basis[:, cols].astype(F32) * (1.0 / 128.0)).astype(BF16)
            part = lax.dot_general(half, data[:, cols], NT, preferred_element_type=F32)
            if h == 0:
                acc[base : base + R] = part
            else:
                acc[base : base + R] += part
    mask_copy.wait()
    mask[...] = ints[...].astype(F32)
    acc[R:] = acc[R:] * mask[...]
    mine, other = halves(place, acc.shape[1] // 2)
    keep[...] = acc[:, mine]
    send[...] = acc[:, other]


def raw_first(place, *whole):
    start_in, start_out, layer_inputs, out_grads, mask = whole
    rows = layer_inputs.shape[0]
    shape = jax.ShapeDtypeStruct((2 * R, rows // 2), F32)
    return pl.pallas_call(
        first_kernel,
        out_shape=(
            shape,
            shape,
            jax.ShapeDtypeStruct(layer_inputs.shape, BF16),
            jax.ShapeDtypeStruct(out_grads.shape, BF16),
            jax.ShapeDtypeStruct(mask.shape, F32),
        ),
        in_specs=[SMEM, HBM, HBM, HBM, HBM, HBM],
        out_specs=(VMEM,) * 5,
        scratch_shapes=[
            pltpu.VMEM(start_in.shape, jnp.int32),
            pltpu.VMEM(start_out.shape, jnp.int32),
            pltpu.VMEM(mask.shape, jnp.int32),
            pltpu.VMEM((2 * R, rows), F32),
            pltpu.SemaphoreType.DMA((8, 4)),
            pltpu.SemaphoreType.DMA,
        ],
        compiler_params=params(8),
        name="raw_first",
    )(place, *(pltpu.with_memory_space_constraint(x, pltpu.HBM) for x in whole))


def half_coords(tokens, img_in, img_out, min_ref, mout_ref, mask, out):
    part = lax.dot_general(img_in, min_ref[tokens, :], NT, preferred_element_type=F32)
    out[:R] = part
    part = lax.dot_general(img_out, mout_ref[tokens, :], NT, preferred_element_type=F32)
    out[R : 2 * R] = part * mask[:, tokens]


def send_kernel(place, img_ref, min_ref, mout_ref, mask, send, img_in, img_out):
    steps = img_ref.shape[1]
    w_in = img_in.shape[1] // steps
    w_out = img_out.shape[1] // steps
    for h in range(steps):
        for g in range(GROUPS):
            rows = slice(g * ROWS, (g + 1) * ROWS)
            img_in[rows, h * w_in : (h + 1) * w_in] = img_ref[g, h, :, :w_in]
            img_out[rows, h * w_out : (h + 1) * w_out] = img_ref[g, h, :, w_in:]
    half_in, half_out = img_in[...], img_out[...]
    _, other = halves(place, send.shape[1])
    half_coords(other, half_in, half_out, min_ref, mout_ref, mask, send)
    gram_in = lax.dot_general(half_in, half_in, NT, preferred_element_type=F32)
    gram_out = lax.dot_general(half_out, half_out, NT, preferred_element_type=F32)
    gram = jnp.concatenate([gram_in, gram_out], axis=1)
    send[2 * R :] = jnp.concatenate([gram[: R // 2], gram[R // 2 :]], axis=1)


def raw_send(place, image, layer_inputs, out_grads, mask):
    rows, d_in = layer_inputs.shape
    d_out = out_grads.shape[1]
    return pl.pallas_call(
        send_kernel,
        out_shape=(
            jax.ShapeDtypeStruct((2 * R + R // 2, rows // 2), F32),
            jax.ShapeDtypeStruct((R, d_in), BF16),
            jax.ShapeDtypeStruct((R, d_out), BF16),
        ),
        in_specs=[SMEM, VMEM, VMEM, VMEM, VMEM],
        out_specs=(VMEM,) * 3,
        compiler_params=params(8),
        name="raw_send",
    )(place, image, layer_inputs, out_grads, mask)


def keep_kernel(place, img_in, img_out, min_ref, mout_ref, mask, keep):
    mine, _ = halves(place, keep.shape[1])
    half_coords(mine, img_in[...], img_out[...], min_ref, mout_ref, mask, keep)


def raw_keep(place, img_in, img_out, layer_inputs, out_grads, mask):
    rows = layer_inputs.shape[0]
    return pl.pallas_call(
        keep_kernel,
        out_shape=jax.ShapeDtypeStruct((2 * R, rows // 2), F32),
        in_specs=[SMEM] + [VMEM] * 5,
        out_specs=VMEM,
        compiler_params=params(8),
        cost_estimate=pl.CostEstimate(flops=1 << 29, bytes_accessed=1 << 22, transcendentals=0),
        name="raw_keep",
    )(place, img_in, img_out, layer_inputs, out_grads, mask)


def near_kernel(keep, *refs):
    *sent, got, near, out = refs
    top = keep.shape[0]
    near[:top] = keep[...] + got[:top]
    out[:top] = near[:top].astype(BF16)
    if sent:
        near[top:] = sent[0][top:] + got[top:]
        out[top:] = split3(near[top:], 0)


def near_of(keep, sent, got):
    top, tokens = keep.shape
    grams = got.shape[0] - top
    return pl.pallas_call(
        near_kernel,
        out_shape=(
            jax.ShapeDtypeStruct(got.shape, F32),
            jax.ShapeDtypeStruct((top + 3 * grams, tokens), BF16),
        ),
        in_specs=[VMEM] * (3 if grams else 2),
        out_specs=(VMEM, VMEM),
        compiler_params=params(4),
        name="near",
    )(keep, *([sent] if grams else []), got)


def whole_raw(near, far):
    return near[: 2 * R] + far[: 2 * R].astype(F32)


def whole_gram(near, far):
    a, b, c = (far[2 * R + i * R // 2 : 2 * R + (i + 1) * R // 2].astype(F32) for i in range(3))
    return near[2 * R :] + (a + b + c)


def coords_kernel(near, far, out):
    out[...] = whole_raw(near, far).astype(BF16)


def coords_of(near, far):
    return pl.pallas_call(
        coords_kernel,
        out_shape=jax.ShapeDtypeStruct(far.shape, BF16),
        in_specs=[VMEM, VMEM],
        out_specs=VMEM,
        compiler_params=params(4),
        name="coords",
    )(near, far)


def image_kernel(place, *refs):
    *parts, mine_ref, other_ref, min_ref, mout_ref, out, coords = refs
    mine, other = halves(place, mine_ref.shape[1])

    @pl.when((place[0] & 1) == 1)
    def _():
        pl.delay(STAGGER_NS)

    for cols, ref in ((mine, mine_ref), (other, other_ref)):
        if parts:
            (inverse,) = parts
            for base, inv in ((0, inverse[:, :R]), (R, inverse[:, R:])):
                coords[base : base + R, cols] = exact_dot(inv, ref[base : base + R]).astype(BF16)
        else:
            coords[:, cols] = ref[...]
    steps = out.shape[1]
    w_in = min_ref.shape[1] // steps
    w_out = mout_ref.shape[1] // steps
    part_in = jnp.dot(coords[:R], min_ref[...], preferred_element_type=F32).astype(BF16)
    part_out = jnp.dot(coords[R:], mout_ref[...], preferred_element_type=F32).astype(BF16)
    for h in range(steps):
        for g in range(GROUPS):
            rows = slice(g * ROWS, (g + 1) * ROWS)
            out[g, h, :, :w_in] = part_in[rows, h * w_in : (h + 1) * w_in]
            out[g, h, :, w_in:] = part_out[rows, h * w_out : (h + 1) * w_out]


def image_of(place, coords, layer_inputs, out_grads):
    steps = 8
    rows, d_in = layer_inputs.shape
    width = (d_in + out_grads.shape[1]) // steps
    return pl.pallas_call(
        image_kernel,
        out_shape=jax.ShapeDtypeStruct((GROUPS, steps, ROWS, width), BF16),
        in_specs=[SMEM] + [VMEM] * (len(coords) + 2),
        out_specs=VMEM,
        scratch_shapes=[pltpu.VMEM((2 * R, rows), BF16)],
        compiler_params=params(8),
        name="image",
    )(place, *coords, layer_inputs, out_grads)


def sum_kernel(parts, out):
    total = parts[0].astype(F32)
    for i in range(1, parts.shape[0]):
        total = total + parts[i].astype(F32)
    half = total.astype(BF16)
    for i in range(parts.shape[0]):
        out[i] = half


def sum_copies(parts):
    return pl.pallas_call(
        sum_kernel,
        out_shape=jax.ShapeDtypeStruct(parts.shape, parts.dtype),
        in_specs=[VMEM],
        out_specs=VMEM,
        compiler_params=params(4),
        name="sum_copies",
    )(parts)


def exact_dot(a, b):
    return jnp.dot(a, b, precision=lax.Precision.HIGHEST, preferred_element_type=F32)


def inverses(gram):
    half = gram.shape[1] // 2
    gram = jnp.concatenate([gram[:, :half], gram[:, half:]], axis=0)
    return eliminate([gram[:, :R], gram[:, R:]])


def total_kernel(near, far, raw, gram):
    raw[...] = whole_raw(near, far)
    gram[...] = whole_gram(near, far)


def total_of(near, far):
    tokens = near.shape[1]
    return pl.pallas_call(
        total_kernel,
        out_shape=tuple(jax.ShapeDtypeStruct((n, tokens), F32) for n in (2 * R, R // 2)),
        in_specs=[VMEM, VMEM],
        out_specs=(VMEM, VMEM),
        compiler_params=params(4),
        name="total",
    )(near, far)


def inverse_kernel(gram, out):
    out[:, :R], out[:, R:] = inverses(gram[...])


def inverse_of(gram):
    return pl.pallas_call(
        inverse_kernel,
        out_shape=jax.ShapeDtypeStruct((R, 2 * R), F32),
        in_specs=[VMEM],
        out_specs=VMEM,
        compiler_params=params(8),
        cost_estimate=pl.CostEstimate(flops=1 << 22, bytes_accessed=1 << 22, transcendentals=0),
        name="inverse",
    )(gram)


def last_kernel(place, inverse, mine, other, img_in, img_out, *refs):
    feat, in_hbm, out_hbm, b_in, b_out, sems = refs
    steps = sems.shape[0]
    copies = []
    for n, (img, own, whole) in enumerate([(img_in, b_in, in_hbm), (img_out, b_out, out_hbm)]):
        split = split3(inverse[:, n * R : (n + 1) * R], 1)
        width = own.shape[1] // steps
        for h in range(steps):
            cols = slice(h * width, (h + 1) * width)
            part = jnp.concatenate([img[:, cols]] * 3, axis=0)
            own[:, cols] = jnp.dot(split, part, preferred_element_type=F32)
            copies.append(
                pltpu.make_async_copy(own.at[:, cols], whole.at[:, cols], sems.at[h, n])
            )
            if len(copies) > 1:
                copies[-2].start()
    copies[-1].start()
    block = feat.shape[1] // R
    inv_in = inverse[pl.ds(pl.multiple_of(place[0] * block, block), block), :][:, :R]
    found = []
    for raw in (mine, other):
        proj_in = exact_dot(inv_in, raw[:R]).astype(BF16)
        proj_out = exact_dot(inverse[:, R:], raw[R:]).astype(BF16)
        one = lax.dot_general(proj_in, proj_out, NT, preferred_element_type=F32) * (1.0 / LEN)
        found.append(jnp.concatenate([one[r : r + 1] for r in range(block)], axis=1))
    even = (place[0] & 1) == 0
    feat[0:1] = jnp.where(even, found[0], found[1])
    feat[1:2] = jnp.where(even, found[1], found[0])
    for copy in copies:
        copy.wait()


def last_of(place, coords, img_in, img_out, count):
    shapes = (img_in.shape, img_out.shape)
    return pl.pallas_call(
        last_kernel,
        out_shape=tuple(jax.ShapeDtypeStruct(s, F32) for s in ((2, R // count * R), *shapes)),
        in_specs=[SMEM] + [VMEM] * 5,
        out_specs=(VMEM, HBM, HBM),
        scratch_shapes=[pltpu.VMEM(s, F32) for s in shapes] + [pltpu.SemaphoreType.DMA((4, 2))],
        compiler_params=params(8),
        name="last",
    )(place, *coords, img_in, img_out)


ORDER = [
    29, 19, 20, 13, 4, 12, 23, 7, 22, 0, 10, 11, 8, 1, 2, 9,
    25, 3, 21, 15, 31, 5, 6, 18, 16, 26, 14, 24, 30, 17, 27, 28,
]
CORE_SWAP = [(0, 1), (1, 0), (2, 3), (3, 2)]
CHIP_SWAP = [(0, 2), (2, 0), (1, 3), (3, 1)]


def shards(layer_inputs, out_grads, loss_mask, start_in, start_out):
    place = lax.axis_index("mp").reshape(1)
    mask = loss_mask.reshape(1, -1)
    send, keep, layer_inputs, out_grads, mask = raw_first(
        place, start_in, start_out, layer_inputs, out_grads, mask
    )
    near, out = near_of(keep, send, lax.ppermute(send, "mp", CORE_SWAP))
    mine = coords_of(near, lax.ppermute(out, "mp", CHIP_SWAP))
    coords = (mine, lax.ppermute(mine, "mp", CORE_SWAP))
    for step in range(ITERS):
        parts = image_of(place, coords, layer_inputs, out_grads)
        grid = parts.shape
        parts = parts.reshape(grid[0] * grid[1], grid[2], grid[3])
        parts = lax.all_to_all(parts, "dp", 0, 0, axis_index_groups=[ORDER])
        image = lax.all_to_all(sum_copies(parts), "dp", 0, 0, axis_index_groups=[ORDER]).reshape(grid)
        send, img_in, img_out = raw_send(place, image, layer_inputs, out_grads, mask)
        got = lax.ppermute(send, "mp", CORE_SWAP)
        keep = raw_keep(place, img_in, img_out, layer_inputs, out_grads, mask)
        near, out = near_of(keep, send, got)
        far = lax.ppermute(out, "mp", CHIP_SWAP)
        raw, gram = total_of(near, far)
        other = lax.ppermute(raw, "mp", CORE_SWAP)
        coords = (inverse_of(gram), raw, other)
    return last_of(place, coords, img_in, img_out, lax.axis_size("mp"))


def solution(mesh):
    in_specs = (P("dp", "mp"), P("dp", "mp"), P("dp"), P(None, "mp"), P(None, "mp"))
    out_specs = (P("dp", "mp"), P(None, "mp"), P(None, "mp"))
    return jax.shard_map(shards, mesh=mesh, in_specs=in_specs, out_specs=out_specs, check_vma=False)
```
